256 devices in a mesh: blk: 128 (over z, y_lo, x, core), col: 2 (over y_hi).
Axes of the slice: x: 4, y: 4 (y_hi: 2, y_lo: 2; y = y_hi * 2 + y_lo), z: 8, core: 2. Of those that a mesh axis runs over, the one named last changes fastest.
Arguments:
- tiles: bfloat16 [3072, 128, 128], P('blk'), may hold values from -0.21875 to 0.21875
- tile_rows: int32 [3072], P('blk'), may hold values from 0 to 3, as said below
- tile_cols: int32 [3072], P('blk'), may hold values from 0 to 511, as said below
- tile_count: int32 [128], P('blk'), may hold values from 3 to 24, as said below
- sketch: bfloat16 [65536, 512], P('blk', 'col'), may hold values from -6 to 6
- variant_scale: bfloat16 [65536], P('blk'), may hold values from 0.5 to 2
Outputs:
- basis_rows: float32 [65536, 512], P('blk', 'col')
The draws below stay inside these ranges and needn't reach their ends.
Inputs may be any that keep to these rules, and one draw needn't show every extreme that they name: `tile_count`: each row group has 24, 12, 6 or 3 live slots, and at least one group has all 24 live. `tile_rows`: no two slots of a row group name the same block row and block column. Slots at or past their group's count are not part of the matrix. `tile_cols`: within one row group, all slots whose block columns lie in the same run of 4 block columns that starts at a multiple of 4 name the same block column.
All inputs are finite; a program needn't handle non-finite values.
Results may differ from the reference program's by a relative error of at most 0.0059.
Values may be sent and summed in bfloat16 or wider, within the bound.
No kernel may reach another device: no remote copies, remote signals or barrier semaphores. Data moves between devices by JAX's collectives and lax.ppermute only.
A program may use at most 128 MiB of HBM per device.

```python
import math
import jax
import jax.numpy as jnp
from jax import lax

BLOCK = 128
K = 512
TPR = 6
RB_DEV = 4
VARIANTS = 65536
TILES = 24
GROUPS = 128
M = 65536


def pattern(key):
    own_blocks = VARIANTS // BLOCK // GROUPS
    exponents = jax.random.randint(jax.random.fold_in(key, 11), (GROUPS,), 0, 4)
    counts = TILES // jnp.left_shift(jnp.ones_like(exponents), exponents)
    chosen = jax.random.randint(jax.random.fold_in(key, 12), (), 0, GROUPS)
    counts = jnp.where(jnp.arange(GROUPS) == chosen, TILES, counts).astype(jnp.int32)
    group_keys = jax.random.split(jax.random.fold_in(key, 13), GROUPS)

    def one_group(group_key):
        picks = jax.random.randint(jax.random.fold_in(group_key, 1), (GROUPS,), 0, own_blocks)
        positions = jax.random.permutation(jax.random.fold_in(group_key, 2), RB_DEV * GROUPS)[:TILES]
        owners = positions % GROUPS
        return (positions // GROUPS, owners * own_blocks + jnp.take(picks, owners))
    row_index, col_index = jax.vmap(one_group)(group_keys)
    return (row_index.reshape(-1).astype(jnp.int32), col_index.reshape(-1).astype(jnp.int32), counts)


def draw_tile_rows(key, part):
    return pattern(key)[0]


def draw_tile_cols(key, part):
    return pattern(key)[1]


def draw_tile_count(key, part):
    return pattern(key)[2]


def block_scale(stream_key, dims, shards, least, high):
    def one(dim, shards_of):
        heights = jax.random.uniform(jax.random.fold_in(jax.random.fold_in(stream_key, 6), dim), (shards_of,), jnp.float32, least / len(shards), high / len(shards))
        return jnp.repeat(jnp.exp(heights), dims[dim] // shards_of).reshape((-1,) + (1,) * (len(dims) - dim - 1))

    gain = one(*shards[0])
    for cut in shards[1:]:
        gain = gain * one(*cut)
    return gain


def scatter_about(own_key, extent, scale, reach, cuts=(), kind=jnp.bfloat16):
    level = block_scale(own_key, extent, cuts, -0.22, 0.18) if cuts else 1.0
    entries = jax.random.normal(own_key, extent, jnp.float32) * scale * level
    return jnp.minimum(jnp.maximum(entries, -reach), reach).astype(kind)


def setup_inputs(seed: int = 0) -> dict:
    key_of = jax.random.split(jax.random.key(seed), 7)
    return {
        "tiles": scatter_about(key_of[0], (GROUPS * TILES, BLOCK, BLOCK), (TPR * BLOCK) ** -0.5, 0.21875, ((0, 128),)),
        "tile_rows": draw_tile_rows(jax.random.fold_in(key_of[6], 71), 0),
        "tile_cols": draw_tile_cols(jax.random.fold_in(key_of[6], 71), 0),
        "tile_count": draw_tile_count(jax.random.fold_in(key_of[6], 71), 0),
        "sketch": scatter_about(key_of[4], (VARIANTS, K), 1.0, 6.0, ((0, 128), (1, 2))),
        "variant_scale": jnp.clip(jnp.exp(math.log(2.0) - 1.3862944 * jax.random.uniform(key_of[5], (VARIANTS,), jnp.float32) ** block_scale(key_of[5], (VARIANTS,), ((0, 128),), -0.2, 0.2)), 0.5, 2.0).astype(jnp.bfloat16),
    }


def reference(tiles, tile_rows, tile_cols, tile_count, sketch, variant_scale):
    col_blocks = VARIANTS // BLOCK
    own_blocks = VARIANTS // BLOCK // GROUPS
    sketch_width = sketch.shape[1]
    tile_groups = tiles.reshape(GROUPS, TILES, BLOCK, BLOCK)
    row_groups = tile_rows.reshape(GROUPS, TILES)
    col_groups = tile_cols.reshape(GROUPS, TILES)
    slot_ids = jnp.arange(TILES, dtype=jnp.int32)
    live_masks = (slot_ids[None, :] < tile_count[:, None]).astype(jnp.float32)
    scales = variant_scale.astype(jnp.float32)
    scaled_sketch = (scales[:, None] * sketch.astype(jnp.float32)).astype(jnp.bfloat16)
    owner_ids = jnp.arange(GROUPS, dtype=jnp.int32)

    def forward(operand):
        blocks = operand.reshape(col_blocks, BLOCK, sketch_width)

        def one_group(pieces):
            tile_group, row_group, col_group, live_mask = pieces
            selected = jnp.take(blocks, col_group, axis=0).astype(jnp.float32)
            products = jnp.einsum('tij,tjk->tik', tile_group.astype(jnp.float32), selected) * live_mask[:, None, None]
            return jnp.zeros((RB_DEV, BLOCK, sketch_width), jnp.float32).at[row_group].add(products)
        result_rows = lax.map(one_group, (tile_groups, row_groups, col_groups, live_masks))
        return result_rows.reshape(GROUPS * RB_DEV * BLOCK, sketch_width)
    range_rows = forward(scaled_sketch).astype(jnp.bfloat16)

    def backward(accumulated, pieces):
        tile_group, row_group, col_group, live_mask, group_rows = pieces
        selected = jnp.take(group_rows, row_group, axis=0).astype(jnp.float32)
        products = jnp.einsum('tji,tjk->tik', tile_group.astype(jnp.float32), selected) * live_mask[:, None, None]
        slot_owner = (col_group // own_blocks).astype(jnp.int32)
        owner_term = jnp.zeros((GROUPS, BLOCK, sketch_width), jnp.float32).at[slot_owner].add(products)
        rounded = lax.optimization_barrier(owner_term.astype(jnp.bfloat16)).astype(jnp.float32)
        slot_hits = (slot_owner[None, :] == owner_ids[:, None]) & (live_mask[None, :] > 0.5)
        wanted = jnp.max(jnp.where(slot_hits, (col_group % own_blocks)[None, :], 0), axis=1).astype(jnp.int32)
        target = (owner_ids * own_blocks + wanted).astype(jnp.int32)
        return (accumulated.at[target].add(rounded), None)
    start_back = jnp.zeros((col_blocks, BLOCK, sketch_width), jnp.float32)
    back, _ = lax.scan(backward, start_back, (tile_groups, row_groups, col_groups, live_masks, range_rows.reshape(GROUPS, RB_DEV, BLOCK, sketch_width)))
    back = back.reshape(VARIANTS, sketch_width)
    weighted = ((scales * scales)[:, None] * back).astype(jnp.bfloat16)
    power_rows = forward(weighted).astype(jnp.bfloat16)
    gram = lax.dot_general(power_rows.astype(jnp.float32), power_rows.astype(jnp.float32), (((0,), (0,)), ((), ())), preferred_element_type=jnp.float32) / M
    lower_factor = jnp.linalg.cholesky(gram)
    identity = jnp.eye(sketch_width, dtype=jnp.float32)
    inverse = jax.scipy.linalg.solve_triangular(lower_factor, identity, lower=True)
    return jnp.dot(power_rows.astype(jnp.float32), inverse.T, precision=lax.Precision.HIGHEST)
```

```python
import jax
import jax.numpy as jnp
from jax import lax
from jax.experimental import pallas as pl
from jax.experimental.pallas import tpu as pltpu
from jax.sharding import PartitionSpec as P

RB_DEV = 4


def spread(rows, axes):
    return lax.all_to_all(rows, axes, split_axis=0, concat_axis=0, tiled=True)


def factor_body(gram_ref, out_ref, work_ref, row_ref):
    edge = row_ref.shape[0]
    size = gram_ref.shape[0]
    count = size // edge
    hi = lax.Precision.HIGHEST
    work_ref[...] = gram_ref[...]
    lanes = lax.broadcasted_iota(jnp.int32, (edge, edge), 1)
    rows = lax.broadcasted_iota(jnp.int32, (edge, edge), 0)

    def stage(k, _):
        base = pl.multiple_of(k * edge, edge)
        w = work_ref[pl.ds(base, edge), pl.ds(base, edge)]
        for j in range(edge):
            row = w[j:j + 1, :]
            r = lax.rsqrt(w[j:j + 1, j:j + 1])
            scaled = jnp.where(lanes[:1] == j, r, row * r)
            first = (j // 8) * 8
            low = w[first:, :]
            below = rows[first:] > j
            factor = jnp.where(below[:, :1], low[:, j:j + 1] * r, 0.0)
            kept = jnp.where(below & (lanes[first:] == j), 0.0, low)
            kept = jnp.where(rows[first:] == j, scaled, kept - factor * scaled)
            w = kept if first == 0 else jnp.concatenate([w[:first], kept], axis=0)
        inv = jnp.where(rows >= lanes, w, 0.0)
        row_ref[...] = jnp.dot(inv, work_ref[pl.ds(base, edge), :], precision=hi, preferred_element_type=jnp.float32)
        row_ref[:, pl.ds(base, edge)] = inv
        work_ref[pl.ds(base, edge), :] = row_ref[...]

        def below_block(i, _):
            at = pl.multiple_of(i * edge, edge)
            work_ref[pl.ds(at, edge), pl.ds(base, edge)] = jnp.zeros((edge, edge), jnp.float32)
            work_ref[pl.ds(at, edge), :] -= lax.dot_general(
                row_ref[:, pl.ds(at, edge)], row_ref[...], (((0,), (0,)), ((), ())),
                precision=hi, preferred_element_type=jnp.float32)
            return 0
        lax.fori_loop(k + 1, count, below_block, 0)
        return 0
    lax.fori_loop(0, count, stage, 0)
    r2 = lax.broadcasted_iota(jnp.int32, (size, size), 0)
    c2 = lax.broadcasted_iota(jnp.int32, (size, size), 1)
    out_ref[...] = jnp.where(r2 >= c2, work_ref[...], 0.0)

def invert_factor(gram):
    n = gram.shape[0]
    return pl.pallas_call(
        factor_body,
        out_shape=jax.ShapeDtypeStruct((n, n), jnp.float32),
        scratch_shapes=[pltpu.VMEM((n, n), jnp.float32), pltpu.VMEM((128, n), jnp.float32)],
    )(gram)


def local(tiles, tile_rows, tile_cols, tile_count, sketch, variant_scale):
    slots, edge, _ = tiles.shape
    width = sketch.shape[1]
    owners = lax.axis_size("blk")
    cols = lax.axis_size("col")
    own_blocks = sketch.shape[0] // edge
    blocks = owners * own_blocks
    bf16, f32 = jnp.bfloat16, jnp.float32

    own_rows = jnp.swapaxes(sketch.reshape(own_blocks, edge, width), 0, 1)
    own_scales = variant_scale.reshape(own_blocks, edge).T
    live = jnp.arange(slots, dtype=jnp.int32) < tile_count[0]
    run = jnp.where(live, tile_cols // own_blocks, -1).astype(bf16)
    member = (tile_cols % own_blocks).astype(bf16)
    notes = jnp.concatenate([run, member])
    notes = jnp.concatenate([own_scales, jnp.broadcast_to(notes, (edge, 2 * slots))], axis=1)
    notes = jnp.pad(notes, ((0, 0), (0, width - notes.shape[1])))
    packed = jnp.concatenate([own_rows, notes[:, None, :]], axis=1)
    kept = spread(packed, "blk")
    kept_rows = kept[:, :own_blocks, :].reshape(blocks, width)
    kept_notes = kept[:, own_blocks, :].astype(f32)
    kept_scale = kept_notes[:, :own_blocks].reshape(blocks, 1)
    all_runs = kept_notes[:, own_blocks : own_blocks + slots]
    all_members = kept_notes[:, own_blocks + slots : own_blocks + 2 * slots]
    all_cols = (all_runs * own_blocks + all_members).astype(jnp.int32)
    block_ids = jnp.arange(blocks, dtype=jnp.int32)
    picks = (all_cols[:, :, None] == block_ids).astype(bf16).reshape(owners * slots, blocks)

    row_ids = jnp.arange(RB_DEV, dtype=jnp.int32)
    row_mask = (tile_rows[:, None] == row_ids).astype(bf16)
    turned = jnp.transpose(tiles, (2, 0, 1))
    wide = turned[:, :, None, :] * row_mask[None, :, :, None]
    wide = wide.reshape(edge * slots, RB_DEV * edge)

    def forward(kept_operand):
        sent = jnp.dot(picks, kept_operand, preferred_element_type=f32).astype(bf16)
        fetched = spread(sent.reshape(owners, slots, width), "blk").reshape(edge * slots, width)
        return lax.dot_general(
            wide, fetched, (((0,), (0,)), ((), ())), preferred_element_type=f32
        ).astype(bf16)

    scaled = (kept_scale * kept_rows.astype(f32)).astype(bf16)
    range_rows = forward(scaled)
    terms = jnp.dot(wide, range_rows, preferred_element_type=f32).astype(bf16)
    arrived = spread(terms.reshape(owners, slots, width), "blk").reshape(owners * slots, width)
    back = lax.dot_general(picks, arrived, (((0,), (0,)), ((), ())), preferred_element_type=f32)
    weighted = ((kept_scale * kept_scale) * back).astype(bf16)
    power_rows = forward(weighted)

    side = lax.axis_index("col")
    other = lax.ppermute(power_rows, "col", [(0, 1), (1, 0)])
    left = jnp.where(side == 0, power_rows, other)
    right = jnp.where(side == 0, other, power_rows)
    all_rows = jnp.concatenate([left, right], axis=1)
    total_rows = all_rows.shape[0] * owners
    half = all_rows.shape[0] // cols
    gram_rows = lax.dynamic_slice_in_dim(all_rows, side * half, half, 0)
    partial = lax.dot_general(
        gram_rows, gram_rows, (((0,), (0,)), ((), ())), preferred_element_type=f32
    )
    everyone = ("blk", "col")
    parts = owners * cols
    share = spread(partial.reshape(parts, -1, edge), everyone).sum(0) / total_rows
    gram_matrix = spread(jnp.broadcast_to(share, (parts,) + share.shape), everyone)
    gram_matrix = gram_matrix.reshape(partial.shape)
    inverse = invert_factor(gram_matrix)
    own_inverse = lax.dynamic_slice_in_dim(inverse, side * width, width, 0)
    return jnp.dot(all_rows.astype(f32), own_inverse.T, precision=lax.Precision.HIGHEST)


def solution(mesh):
    placed = (P("blk", None, None), P("blk"), P("blk"), P("blk"), P("blk", "col"), P("blk"))
    return jax.shard_map(
        local, mesh=mesh, in_specs=placed, out_specs=P("blk", "col"), check_vma=False
    )
```

```python
import jax
import jax.numpy as jnp
from jax import lax
from jax.experimental import pallas as pl
from jax.experimental.pallas import tpu as pltpu
from jax.sharding import Mesh
from jax.sharding import PartitionSpec as P

RB_DEV = 4
STREAMS = 2
GROUPS = ("z", "y", "x", "core")
NEAR = ("x", "core")
FAR = ("z", "y", "col")


def spread(rows, axes):
    return lax.all_to_all(rows, axes, split_axis=0, concat_axis=0, tiled=True)


SUB = 8
F32 = jnp.float32


def eliminate(rows, edge):
    lane = lax.broadcasted_iota(jnp.int32, (SUB, edge), 1)
    sub = lax.broadcasted_iota(jnp.int32, (SUB, edge), 0)
    rows = list(rows)
    last = len(rows)
    for g in range(last):
        base = g * SUB
        inside = (lane >= base) & (lane < base + SUB)
        start = jnp.where(inside, jnp.where(lane - base == sub, 1.0, 0.0), rows[g])
        columns = [jnp.broadcast_to(rows[g][:, base + c : base + c + 1], (SUB, edge)) for c in range(SUB)]
        s = {(a, c): jnp.broadcast_to(columns[c][a : a + 1, :], (SUB, edge)) for a in range(SUB) for c in range(a, SUB)}
        x = [jnp.broadcast_to(start[a : a + 1, :], (SUB, edge)) for a in range(SUB)]
        r, low = [], {}
        ahead = g + 1 < last
        if ahead:
            nxt = rows[g + 1]
            fac = [jnp.broadcast_to(nxt[:, base + c : base + c + 1], (SUB, edge)) for c in range(SUB)]
            nxt = jnp.where(inside, 0.0, nxt)
        for a in range(SUB):
            r.append(lax.rsqrt(s[a, a]))
            for c in range(a + 1, SUB):
                low[c, a] = s[a, c] * r[a]
            for c in range(a + 1, SUB):
                for e in range(c, SUB):
                    s[c, e] = s[c, e] - low[c, a] * low[e, a]
            x[a] = x[a] * r[a]
            if ahead:
                fac[a] = fac[a] * r[a]
                nxt = nxt - fac[a] * x[a]
            for c in range(a + 1, SUB):
                x[c] = x[c] - low[c, a] * x[a]
                if ahead:
                    fac[c] = fac[c] - fac[a] * low[c, a]
        done = x[0]
        for a in range(1, SUB):
            done = jnp.where(sub == a, x[a], done)
        if g + 2 < last:
            z = [None] * SUB
            for a in range(SUB - 1, -1, -1):
                t = x[a]
                for c in range(a + 1, SUB):
                    t = t - low[c, a] * z[c]
                z[a] = t * r[a]
            for h in range(g + 2, last):
                old = rows[h]
                t = jnp.where(inside, 0.0, old)
                for a in range(SUB):
                    t = t - jnp.broadcast_to(old[:, base + a : base + a + 1], (SUB, edge)) * z[a]
                rows[h] = t
        if ahead:
            rows[g + 1] = nxt
        rows[g] = done
    return rows


def factor_body(gram_ref, out_ref, work_ref, row_ref):
    edge = row_ref.shape[0]
    size = out_ref.shape[0]
    count = size // edge
    hi = lax.Precision.HIGHEST
    n = 0
    for i in range(count):
        for j in range(i, count):
            work_ref[i * edge : (i + 1) * edge, j * edge : (j + 1) * edge] = gram_ref[n * edge : (n + 1) * edge, :]
            n += 1
    for i in range(1, count):
        work_ref[i * edge : (i + 1) * edge, : i * edge] = jnp.zeros((edge, i * edge), F32)

    def stage(k, carry):
        base = pl.multiple_of(k * edge, edge)
        rows = [work_ref[pl.ds(base + SUB * h, SUB), pl.ds(base, edge)] for h in range(edge // SUB)]
        w = jnp.concatenate(eliminate(rows, edge), axis=0)
        r2 = lax.broadcasted_iota(jnp.int32, (edge, edge), 0)
        c2 = lax.broadcasted_iota(jnp.int32, (edge, edge), 1)
        inv = jnp.where(r2 >= c2, w, 0.0)
        row_ref[...] = jnp.dot(inv, work_ref[pl.ds(base, edge), :], precision=hi, preferred_element_type=F32)
        row_ref[:, pl.ds(base, edge)] = inv
        work_ref[pl.ds(base, edge), :] = row_ref[...]

        def below(i, carry):
            at = pl.multiple_of(i * edge, edge)
            work_ref[pl.ds(at, edge), pl.ds(base, edge)] = jnp.zeros((edge, edge), F32)
            work_ref[pl.ds(at, edge), :] -= lax.dot_general(
                row_ref[:, pl.ds(at, edge)], row_ref[...], (((0,), (0,)), ((), ())),
                precision=hi, preferred_element_type=F32)
            return carry

        return lax.fori_loop(k + 1, count, below, carry)

    lax.fori_loop(0, count, stage, 0)
    out_ref[...] = work_ref[...]
    for i in range(count):
        if i + 1 < count:
            out_ref[i * edge : (i + 1) * edge, (i + 1) * edge :] = jnp.zeros((edge, size - (i + 1) * edge), F32)


def invert_factor(packed, size):
    edge = packed.shape[1]
    return pl.pallas_call(
        factor_body,
        out_shape=jax.ShapeDtypeStruct((size, size), F32),
        scratch_shapes=[pltpu.VMEM((size, size), F32), pltpu.VMEM((edge, size), F32)],
    )(packed)


def gram_body(side_ref, mine_ref, other_ref, packed_ref):
    edge = packed_ref.shape[1]
    width = mine_ref.shape[1]
    half = mine_ref.shape[0] // 2
    side = side_ref[0]
    at = pl.multiple_of(side * half, half)
    mine = mine_ref[pl.ds(at, half), :]
    other = other_ref[pl.ds(at, half), :]
    left = jnp.where(side == 0, mine, other)
    right = jnp.where(side == 0, other, mine)

    def product(a, b):
        return lax.dot_general(a, b, (((0,), (0,)), ((), ())), preferred_element_type=F32)

    per = width // edge
    both = (product(left, left), product(left, right), product(right, right))
    n = 0
    for i in range(2 * per):
        for j in range(i, 2 * per):
            piece = both[i // per + j // per]
            a, b = i % per * edge, j % per * edge
            packed_ref[n * edge : (n + 1) * edge, :] = piece[a : a + edge, b : b + edge]
            n += 1


def upper_gram(side, mine, other, edge):
    count = 2 * mine.shape[1] // edge
    return pl.pallas_call(
        gram_body,
        out_shape=jax.ShapeDtypeStruct((count * (count + 1) // 2 * edge, edge), F32),
        in_specs=[pl.BlockSpec(memory_space=pltpu.SMEM)] + [pl.BlockSpec(memory_space=pltpu.VMEM)] * 2,
        out_specs=pl.BlockSpec(memory_space=pltpu.VMEM),
    )(side, mine, other)


def local(tiles, tile_rows, tile_cols, tile_count, sketch, variant_scale):
    slots, edge, _ = tiles.shape
    width = sketch.shape[1]
    owners = lax.axis_size(GROUPS)
    cols = lax.axis_size("col")
    own_blocks = sketch.shape[0] // edge
    blocks = owners * own_blocks
    bf16, f32 = jnp.bfloat16, jnp.float32

    own_rows = jnp.swapaxes(sketch.reshape(own_blocks, edge, width), 0, 1)
    own_scales = variant_scale.reshape(own_blocks, edge).T
    live = jnp.arange(slots, dtype=jnp.int32) < tile_count[0]
    run = jnp.where(live, tile_cols // own_blocks, -1).astype(bf16)
    member = (tile_cols % own_blocks).astype(bf16)
    notes = jnp.concatenate([run, member])
    notes = jnp.concatenate([own_scales, jnp.broadcast_to(notes, (edge, 2 * slots))], axis=1)
    notes = jnp.pad(notes, ((0, 0), (0, width - notes.shape[1])))
    packed = jnp.concatenate([own_rows, notes[:, None, :]], axis=1)
    kept = spread(packed, GROUPS)
    kept_rows = kept[:, :own_blocks, :].reshape(blocks, width)
    kept_notes = kept[:, own_blocks, :].astype(f32)
    kept_scale = kept_notes[:, :own_blocks].reshape(blocks, 1)
    all_runs = kept_notes[:, own_blocks : own_blocks + slots]
    all_members = kept_notes[:, own_blocks + slots : own_blocks + 2 * slots]
    all_cols = (all_runs * own_blocks + all_members).astype(jnp.int32)
    block_ids = jnp.arange(blocks, dtype=jnp.int32)
    picks = (all_cols[:, :, None] == block_ids).astype(bf16).reshape(owners * slots, blocks)

    row_ids = jnp.arange(RB_DEV, dtype=jnp.int32)
    row_mask = (tile_rows[:, None] == row_ids).astype(bf16)
    turned = jnp.transpose(tiles, (2, 0, 1))
    wide = turned[:, :, None, :] * row_mask[None, :, :, None]
    wide = wide.reshape(edge * slots, RB_DEV * edge)

    def forward(kept_operand):
        sent = jnp.dot(picks, kept_operand, preferred_element_type=f32).astype(bf16)
        fetched = spread(sent.reshape(owners, slots, -1), GROUPS).reshape(edge * slots, -1)
        return lax.dot_general(
            wide, fetched, (((0,), (0,)), ((), ())), preferred_element_type=f32
        ).astype(bf16)

    def power(kept_part):
        scaled = (kept_scale * kept_part.astype(f32)).astype(bf16)
        range_rows = forward(scaled)
        terms = jnp.dot(wide, range_rows, preferred_element_type=f32).astype(bf16)
        arrived = spread(terms.reshape(owners, slots, -1), GROUPS).reshape(owners * slots, -1)
        back = lax.dot_general(picks, arrived, (((0,), (0,)), ((), ())), preferred_element_type=f32)
        weighted = ((kept_scale * kept_scale) * back).astype(bf16)
        return forward(weighted)

    piece = width // STREAMS
    power_rows = jnp.concatenate(
        [power(kept_rows[:, at : at + piece]) for at in range(0, width, piece)], axis=1
    )

    side = lax.axis_index("col")
    other = lax.ppermute(power_rows, "col", [(0, 1), (1, 0)])
    packed_gram = upper_gram(side.reshape(1), power_rows, other, edge)
    left = jnp.where(side == 0, power_rows, other)
    right = jnp.where(side == 0, other, power_rows)
    all_rows = jnp.concatenate([left, right], axis=1)
    total_rows = all_rows.shape[0] * owners
    near, far = lax.axis_size(NEAR), lax.axis_size(FAR)
    near_share = spread(packed_gram.reshape(near, -1, edge), NEAR).sum(0)
    share = spread(near_share.reshape(far, -1, edge), FAR).sum(0) / total_rows
    near_share = spread(jnp.broadcast_to(share, (far,) + share.shape), FAR).reshape(-1, edge)
    summed = spread(jnp.broadcast_to(near_share, (near,) + near_share.shape), NEAR)
    inverse = invert_factor(summed.reshape(-1, edge), width * cols)
    own_inverse = lax.dynamic_slice_in_dim(inverse, side * width, width, 0)
    return jnp.dot(all_rows.astype(f32), own_inverse.T, precision=lax.Precision.HIGHEST)


def solution(mesh):
    owners, cols = mesh.devices.shape
    fine = Mesh(mesh.devices.reshape(owners // 16, 2, 4, 2, cols), GROUPS + ("col",))
    grouped = P(GROUPS)
    placed = (P(GROUPS, None, None), grouped, grouped, grouped, P(GROUPS, "col"), grouped)
    return jax.shard_map(
        local, mesh=fine, in_specs=placed, out_specs=P(GROUPS, "col"), check_vma=False
    )
```

```python
import jax
import jax.numpy as jnp
from jax import lax
from jax.experimental import pallas as pl
from jax.experimental.pallas import tpu as pltpu
from jax.sharding import Mesh
from jax.sharding import PartitionSpec as P

RB_DEV = 4
GROUPS = ("z", "y", "x", "core")


def spread(rows, axes):
    return lax.all_to_all(rows, axes, split_axis=0, concat_axis=0, tiled=True)


SUB = 8
F32 = jnp.float32


def block_places():
    own = [((0, 0), (0, 1), (1, 1)), ((2, 2), (2, 3), (3, 3))]
    cross = [((0, 2), (1, 2)), ((0, 3), (1, 3))]
    return [place for side in range(2) for place in own[side] + cross[side]]


def eliminate(rows, edge):
    lane = lax.broadcasted_iota(jnp.int32, (SUB, edge), 1)
    sub = lax.broadcasted_iota(jnp.int32, (SUB, edge), 0)
    rows = list(rows)
    last = len(rows)
    for g in range(last):
        base = g * SUB
        inside = (lane >= base) & (lane < base + SUB)
        start = jnp.where(inside, jnp.where(lane - base == sub, 1.0, 0.0), rows[g])
        columns = [jnp.broadcast_to(rows[g][:, base + c : base + c + 1], (SUB, edge)) for c in range(SUB)]
        s = {(a, c): jnp.broadcast_to(columns[c][a : a + 1, :], (SUB, edge)) for a in range(SUB) for c in range(a, SUB)}
        x = [jnp.broadcast_to(start[a : a + 1, :], (SUB, edge)) for a in range(SUB)]
        r, low = [], {}
        ahead = g + 1 < last
        if ahead:
            nxt = rows[g + 1]
            fac = [jnp.broadcast_to(nxt[:, base + c : base + c + 1], (SUB, edge)) for c in range(SUB)]
            nxt = jnp.where(inside, 0.0, nxt)
        for a in range(SUB):
            r.append(lax.rsqrt(s[a, a]))
            for c in range(a + 1, SUB):
                low[c, a] = s[a, c] * r[a]
            for c in range(a + 1, SUB):
                for e in range(c, SUB):
                    s[c, e] = s[c, e] - low[c, a] * low[e, a]
            x[a] = x[a] * r[a]
            if ahead:
                fac[a] = fac[a] * r[a]
                nxt = nxt - fac[a] * x[a]
            for c in range(a + 1, SUB):
                x[c] = x[c] - low[c, a] * x[a]
                if ahead:
                    fac[c] = fac[c] - fac[a] * low[c, a]
        done = x[0]
        for a in range(1, SUB):
            done = jnp.where(sub == a, x[a], done)
        if g + 2 < last:
            z = [None] * SUB
            for a in range(SUB - 1, -1, -1):
                t = x[a]
                for c in range(a + 1, SUB):
                    t = t - low[c, a] * z[c]
                z[a] = t * r[a]
            for h in range(g + 2, last):
                old = rows[h]
                t = jnp.where(inside, 0.0, old)
                for a in range(SUB):
                    t = t - jnp.broadcast_to(old[:, base + a : base + a + 1], (SUB, edge)) * z[a]
                rows[h] = t
        if ahead:
            rows[g + 1] = nxt
        rows[g] = done
    return rows


def factor_body(gram_ref, out_ref, work_ref, row_ref):
    edge = row_ref.shape[0]
    size = out_ref.shape[0]
    count = size // edge
    hi = lax.Precision.HIGHEST
    for n, (i, j) in enumerate(block_places()):
        work_ref[i * edge : (i + 1) * edge, j * edge : (j + 1) * edge] = gram_ref[:, n * edge : (n + 1) * edge]
    for i in range(1, count):
        work_ref[i * edge : (i + 1) * edge, : i * edge] = jnp.zeros((edge, i * edge), F32)

    def stage(k, carry):
        base = pl.multiple_of(k * edge, edge)
        rows = [work_ref[pl.ds(base + SUB * h, SUB), pl.ds(base, edge)] for h in range(edge // SUB)]
        w = jnp.concatenate(eliminate(rows, edge), axis=0)
        r2 = lax.broadcasted_iota(jnp.int32, (edge, edge), 0)
        c2 = lax.broadcasted_iota(jnp.int32, (edge, edge), 1)
        inv = jnp.where(r2 >= c2, w, 0.0)
        row_ref[...] = jnp.dot(inv, work_ref[pl.ds(base, edge), :], precision=hi, preferred_element_type=F32)
        row_ref[:, pl.ds(base, edge)] = inv
        work_ref[pl.ds(base, edge), :] = row_ref[...]

        def below(i, carry):
            at = pl.multiple_of(i * edge, edge)
            work_ref[pl.ds(at, edge), pl.ds(base, edge)] = jnp.zeros((edge, edge), F32)
            work_ref[pl.ds(at, edge), :] -= lax.dot_general(
                row_ref[:, pl.ds(at, edge)], row_ref[...], (((0,), (0,)), ((), ())),
                precision=hi, preferred_element_type=F32)
            return carry

        return lax.fori_loop(k + 1, count, below, carry)

    lax.fori_loop(0, count, stage, 0)
    out_ref[...] = work_ref[...]
    for i in range(count):
        if i + 1 < count:
            out_ref[i * edge : (i + 1) * edge, (i + 1) * edge :] = jnp.zeros((edge, size - (i + 1) * edge), F32)


def invert_factor(packed, size):
    edge = packed.shape[0]
    return pl.pallas_call(
        factor_body,
        out_shape=jax.ShapeDtypeStruct((size, size), F32),
        scratch_shapes=[pltpu.VMEM((size, size), F32), pltpu.VMEM((edge, size), F32)],
    )(packed)


def gram_body(side_ref, mine_ref, other_ref, packed_ref):
    edge = packed_ref.shape[0]
    first = side_ref[0] == 0
    mine = mine_ref[...]
    other = other_ref[...]
    left = jnp.where(first, mine, other)
    right = jnp.where(first, other[:, :edge], mine[:, edge:])

    def product(a, b):
        return lax.dot_general(a, b, (((0,), (0,)), ((), ())), preferred_element_type=F32)

    own = product(mine, mine)
    cross = product(left, right)
    pieces = (own[:edge, :edge], own[:edge, edge:], own[edge:, edge:], cross[:edge], cross[edge:])
    for n, piece in enumerate(pieces):
        packed_ref[:, n * edge : (n + 1) * edge] = piece


def pair_gram(side, mine, other, edge):
    return pl.pallas_call(
        gram_body,
        out_shape=jax.ShapeDtypeStruct((edge, 5 * edge), F32),
        in_specs=[pl.BlockSpec(memory_space=pltpu.SMEM)] + [pl.BlockSpec(memory_space=pltpu.VMEM)] * 2,
        out_specs=pl.BlockSpec(memory_space=pltpu.VMEM),
    )(side, mine, other)


def local(tiles, tile_rows, tile_cols, tile_count, sketch, variant_scale):
    slots, edge, _ = tiles.shape
    width = sketch.shape[1]
    owners = lax.axis_size(GROUPS)
    cols = lax.axis_size("col")
    own_blocks = sketch.shape[0] // edge
    blocks = owners * own_blocks
    bf16, f32 = jnp.bfloat16, jnp.float32

    own_rows = jnp.swapaxes(sketch.reshape(own_blocks, edge, width), 0, 1)
    own_scales = variant_scale.reshape(own_blocks, edge).T
    live = jnp.arange(slots, dtype=jnp.int32) < tile_count[0]
    run = jnp.where(live, tile_cols // own_blocks, -1).astype(bf16)
    member = (tile_cols % own_blocks).astype(bf16)
    notes = jnp.concatenate([run, member])
    notes = jnp.concatenate([own_scales, jnp.broadcast_to(notes, (edge, 2 * slots))], axis=1)
    notes = jnp.pad(notes, ((0, 0), (0, width - notes.shape[1])))
    packed = jnp.concatenate([own_rows, notes[:, None, :]], axis=1)
    kept = spread(packed, GROUPS)
    kept_rows = kept[:, :own_blocks, :].reshape(blocks, width)
    kept_notes = kept[:, own_blocks, :].astype(f32)
    kept_scale = kept_notes[:, :own_blocks].reshape(blocks, 1)
    all_runs = kept_notes[:, own_blocks : own_blocks + slots]
    all_members = kept_notes[:, own_blocks + slots : own_blocks + 2 * slots]
    all_cols = (all_runs * own_blocks + all_members).astype(jnp.int32)
    block_ids = jnp.arange(blocks, dtype=jnp.int32)
    picks = (all_cols[:, :, None] == block_ids).astype(bf16).reshape(owners * slots, blocks)

    row_ids = jnp.arange(RB_DEV, dtype=jnp.int32)
    row_mask = (tile_rows[:, None] == row_ids).astype(bf16)
    turned = jnp.transpose(tiles, (2, 0, 1))
    wide = turned[:, :, None, :] * row_mask[None, :, :, None]
    wide = wide.reshape(edge * slots, RB_DEV * edge)

    def forward(kept_operand):
        sent = jnp.dot(picks, kept_operand, preferred_element_type=f32).astype(bf16)
        fetched = spread(sent.reshape(owners, slots, width), GROUPS).reshape(edge * slots, width)
        return lax.dot_general(
            wide, fetched, (((0,), (0,)), ((), ())), preferred_element_type=f32
        ).astype(bf16)

    scaled = (kept_scale * kept_rows.astype(f32)).astype(bf16)
    range_rows = lax.optimization_barrier(forward(scaled))
    terms = jnp.dot(wide, range_rows, preferred_element_type=f32).astype(bf16)
    arrived = spread(terms.reshape(owners, slots, width), GROUPS).reshape(owners * slots, width)
    back = lax.dot_general(picks, arrived, (((0,), (0,)), ((), ())), preferred_element_type=f32)
    weighted = ((kept_scale * kept_scale) * back).astype(bf16)
    power_rows = forward(lax.optimization_barrier(weighted))

    side = lax.axis_index("col")
    other = lax.ppermute(power_rows, "col", [(0, 1), (1, 0)])
    packed_gram = pair_gram(side.reshape(1), power_rows, other, edge)
    left = jnp.where(side == 0, power_rows, other)
    right = jnp.where(side == 0, other, power_rows)
    all_rows = jnp.concatenate([left, right], axis=1)
    total_rows = all_rows.shape[0] * owners
    share = spread(packed_gram.reshape(owners, 1, -1), GROUPS).sum(0) / total_rows
    summed = spread(jnp.broadcast_to(share, (owners * cols,) + share.shape), GROUPS + ("col",))
    inverse = invert_factor(summed.reshape(owners, -1), width * cols)
    own_inverse = lax.dynamic_slice_in_dim(inverse, side * width, width, 0)
    return jnp.dot(all_rows.astype(f32), own_inverse.T, precision=lax.Precision.HIGHEST)


def solution(mesh):
    owners, cols = mesh.devices.shape
    fine = Mesh(mesh.devices.reshape(owners // 16, 2, 4, 2, cols), GROUPS + ("col",))
    grouped = P(GROUPS)
    placed = (P(GROUPS, None, None), grouped, grouped, grouped, P(GROUPS, "col"), grouped)
    return jax.shard_map(
        local, mesh=fine, in_specs=placed, out_specs=P(GROUPS, "col"), check_vma=False
    )
```

```python
import jax
import jax.numpy as jnp
from jax import lax
from jax.experimental import pallas as pl
from jax.experimental.pallas import tpu as pltpu
from jax.sharding import Mesh
from jax.sharding import PartitionSpec as P

RB_DEV = 4
CHIPS = ("z", "y", "x")
GROUPS = CHIPS + ("core",)


def spread(rows, axes):
    return lax.all_to_all(rows, axes, split_axis=0, concat_axis=0, tiled=True)


SUB = 8
F32 = jnp.float32


def block_places():
    own = [((0, 0), (0, 1), (1, 1)), ((2, 2), (2, 3), (3, 3))]
    cross = [((0, 2), (1, 2)), ((0, 3), (1, 3))]
    return [place for side in range(2) for place in own[side] + cross[side]]


def eliminate(rows, edge):
    lane = lax.broadcasted_iota(jnp.int32, (SUB, edge), 1)
    sub = lax.broadcasted_iota(jnp.int32, (SUB, edge), 0)
    rows = list(rows)
    last = len(rows)
    for g in range(last):
        base = g * SUB
        inside = (lane >= base) & (lane < base + SUB)
        start = jnp.where(inside, jnp.where(lane - base == sub, 1.0, 0.0), rows[g])
        columns = [jnp.broadcast_to(rows[g][:, base + c : base + c + 1], (SUB, edge)) for c in range(SUB)]
        s = {(a, c): jnp.broadcast_to(columns[c][a : a + 1, :], (SUB, edge)) for a in range(SUB) for c in range(a, SUB)}
        x = [jnp.broadcast_to(start[a : a + 1, :], (SUB, edge)) for a in range(SUB)]
        r, low = [], {}
        ahead = g + 1 < last
        if ahead:
            nxt = rows[g + 1]
            fac = [jnp.broadcast_to(nxt[:, base + c : base + c + 1], (SUB, edge)) for c in range(SUB)]
            nxt = jnp.where(inside, 0.0, nxt)
        for a in range(SUB):
            r.append(lax.rsqrt(s[a, a]))
            for c in range(a + 1, SUB):
                low[c, a] = s[a, c] * r[a]
            for c in range(a + 1, SUB):
                for e in range(c, SUB):
                    s[c, e] = s[c, e] - low[c, a] * low[e, a]
            x[a] = x[a] * r[a]
            if ahead:
                fac[a] = fac[a] * r[a]
                nxt = nxt - fac[a] * x[a]
            for c in range(a + 1, SUB):
                x[c] = x[c] - low[c, a] * x[a]
                if ahead:
                    fac[c] = fac[c] - fac[a] * low[c, a]
        done = x[0]
        for a in range(1, SUB):
            done = jnp.where(sub == a, x[a], done)
        if g + 2 < last:
            z = [None] * SUB
            for a in range(SUB - 1, -1, -1):
                t = x[a]
                for c in range(a + 1, SUB):
                    t = t - low[c, a] * z[c]
                z[a] = t * r[a]
            for h in range(g + 2, last):
                old = rows[h]
                t = jnp.where(inside, 0.0, old)
                for a in range(SUB):
                    t = t - jnp.broadcast_to(old[:, base + a : base + a + 1], (SUB, edge)) * z[a]
                rows[h] = t
        if ahead:
            rows[g + 1] = nxt
        rows[g] = done
    return rows


def basis_body(ids_ref, own_ref, twin_ref, mine_ref, other_ref, out_ref, work_ref, row_ref, mix_ref):
    edge, size = row_ref.shape
    count = size // edge
    hi = lax.Precision.HIGHEST
    part = own_ref.shape[0]
    core = ids_ref[1]
    for n, (i, j) in enumerate(block_places()):
        lanes = slice(n * edge, (n + 1) * edge)
        mix_ref[pl.ds(n * edge + core, part, 2), :] = own_ref[:, lanes]
        mix_ref[pl.ds(n * edge + 1 - core, part, 2), :] = twin_ref[:, lanes]
        work_ref[i * edge : (i + 1) * edge, j * edge : (j + 1) * edge] = mix_ref[n * edge : (n + 1) * edge, :]
    for i in range(1, count):
        work_ref[i * edge : (i + 1) * edge, : i * edge] = jnp.zeros((edge, i * edge), F32)

    def stage(k, carry):
        base = pl.multiple_of(k * edge, edge)
        rows = [work_ref[pl.ds(base + SUB * h, SUB), pl.ds(base, edge)] for h in range(edge // SUB)]
        w = jnp.concatenate(eliminate(rows, edge), axis=0)
        r2 = lax.broadcasted_iota(jnp.int32, (edge, edge), 0)
        c2 = lax.broadcasted_iota(jnp.int32, (edge, edge), 1)
        inv = jnp.where(r2 >= c2, w, 0.0)
        row_ref[...] = jnp.dot(inv, work_ref[pl.ds(base, edge), :], precision=hi, preferred_element_type=F32)
        row_ref[:, pl.ds(base, edge)] = inv
        work_ref[pl.ds(base, edge), :] = row_ref[...]

        def below(i, carry):
            at = pl.multiple_of(i * edge, edge)
            work_ref[pl.ds(at, edge), pl.ds(base, edge)] = jnp.zeros((edge, edge), F32)
            work_ref[pl.ds(at, edge), :] -= lax.dot_general(
                row_ref[:, pl.ds(at, edge)], row_ref[...], (((0,), (0,)), ((), ())),
                precision=hi, preferred_element_type=F32)
            return carry

        return lax.fori_loop(k + 1, count, below, carry)

    lax.fori_loop(0, count, stage, 0)
    for i in range(count - 1):
        work_ref[i * edge : (i + 1) * edge, (i + 1) * edge :] = jnp.zeros((edge, size - (i + 1) * edge), F32)
    width = mine_ref.shape[1]
    first = ids_ref[0] == 0
    left = jnp.where(first, mine_ref[...], other_ref[...])
    right = jnp.where(first, other_ref[...], mine_ref[...])
    rest = work_ref[pl.ds(pl.multiple_of(ids_ref[0] * width, width), width), :]
    total = jnp.zeros(out_ref.shape, F32)
    for _ in range(3):
        step = rest.astype(jnp.bfloat16)
        rest = rest - step.astype(F32)
        for at, rows in ((0, left), (width, right)):
            total += lax.dot_general(
                rows, step[:, at : at + width], (((1,), (1,)), ((), ())), preferred_element_type=F32
            )
    out_ref[...] = total


def basis(ids, own, twin, mine, other):
    edge, size = 2 * own.shape[0], 2 * mine.shape[1]
    return pl.pallas_call(
        basis_body,
        out_shape=jax.ShapeDtypeStruct(mine.shape, F32),
        in_specs=[pl.BlockSpec(memory_space=pltpu.SMEM)] + [pl.BlockSpec(memory_space=pltpu.VMEM)] * 4,
        out_specs=pl.BlockSpec(memory_space=pltpu.VMEM),
        scratch_shapes=[pltpu.VMEM((size, size), F32), pltpu.VMEM((edge, size), F32), pltpu.VMEM((own.size // edge * 2, edge), F32)],
    )(ids, own, twin, mine, other)


def gram_body(side_ref, mine_ref, other_ref, packed_ref):
    edge = packed_ref.shape[0]
    first = side_ref[0] == 0
    mine = mine_ref[...]
    other = other_ref[...]
    left = jnp.where(first, mine, other)
    right = jnp.where(first, other[:, :edge], mine[:, edge:])

    def product(a, b):
        return lax.dot_general(a, b, (((0,), (0,)), ((), ())), preferred_element_type=F32)

    own = product(mine, mine)
    cross = product(left, right)
    pieces = (own[:edge, :edge], own[:edge, edge:], own[edge:, edge:], cross[:edge], cross[edge:])
    for n, piece in enumerate(pieces):
        packed_ref[:, n * edge : (n + 1) * edge] = piece


def pair_gram(side, mine, other, edge):
    return pl.pallas_call(
        gram_body,
        out_shape=jax.ShapeDtypeStruct((edge, 5 * edge), F32),
        in_specs=[pl.BlockSpec(memory_space=pltpu.SMEM)] + [pl.BlockSpec(memory_space=pltpu.VMEM)] * 2,
        out_specs=pl.BlockSpec(memory_space=pltpu.VMEM),
    )(side, mine, other)


def local(tiles, tile_rows, tile_cols, tile_count, sketch, variant_scale):
    slots, edge, _ = tiles.shape
    width = sketch.shape[1]
    owners = lax.axis_size(GROUPS)
    cols = lax.axis_size("col")
    own_blocks = sketch.shape[0] // edge
    blocks = owners * own_blocks
    bf16, f32 = jnp.bfloat16, jnp.float32

    own_rows = jnp.swapaxes(sketch.reshape(own_blocks, edge, width), 0, 1)
    own_scales = variant_scale.reshape(own_blocks, edge).T
    live = jnp.arange(slots, dtype=jnp.int32) < tile_count[0]
    run = jnp.where(live, tile_cols // own_blocks, -1).astype(bf16)
    member = (tile_cols % own_blocks).astype(bf16)
    notes = jnp.concatenate([run, member])
    notes = jnp.concatenate([own_scales, jnp.broadcast_to(notes, (edge, 2 * slots))], axis=1)
    notes = jnp.pad(notes, ((0, 0), (0, width - notes.shape[1])))
    packed = jnp.concatenate(
        [own_rows.reshape(edge, 2, -1), notes.reshape(edge, 2, -1)], axis=2
    )
    kept = spread(packed, GROUPS)
    row_part = own_blocks // 2 * width
    kept_rows = kept[:, :, :row_part].reshape(blocks, width)
    kept_notes = kept[:, :, row_part:].reshape(owners, width).astype(f32)
    kept_scale = kept_notes[:, :own_blocks].reshape(blocks, 1)
    all_runs = kept_notes[:, own_blocks : own_blocks + slots]
    all_members = kept_notes[:, own_blocks + slots : own_blocks + 2 * slots]
    all_cols = (all_runs * own_blocks + all_members).astype(jnp.int32)
    block_ids = jnp.arange(blocks, dtype=jnp.int32)
    picks = (all_cols[:, :, None] == block_ids).astype(bf16).reshape(owners * slots, blocks)

    row_ids = jnp.arange(RB_DEV, dtype=jnp.int32)
    row_mask = (tile_rows[:, None] == row_ids).astype(bf16)
    turned = jnp.transpose(tiles, (2, 0, 1))
    wide = turned[:, :, None, :] * row_mask[None, :, :, None]
    wide = wide.reshape(edge * slots, RB_DEV * edge)

    def forward(kept_operand):
        sent = jnp.dot(picks, kept_operand, preferred_element_type=f32).astype(bf16)
        fetched = spread(sent.reshape(owners, slots, width), GROUPS).reshape(edge * slots, width)
        return lax.dot_general(
            wide, fetched, (((0,), (0,)), ((), ())), preferred_element_type=f32
        ).astype(bf16)

    scaled = (kept_scale * kept_rows.astype(f32)).astype(bf16)
    range_rows = lax.optimization_barrier(forward(scaled))
    terms = jnp.dot(wide, range_rows, preferred_element_type=f32).astype(bf16)
    arrived = spread(terms.reshape(owners, slots, width), GROUPS).reshape(owners * slots, width)
    back = lax.dot_general(picks, arrived, (((0,), (0,)), ((), ())), preferred_element_type=f32)
    weighted = ((kept_scale * kept_scale) * back).astype(bf16)
    power_rows = forward(lax.optimization_barrier(weighted))

    side = lax.axis_index("col")
    other = lax.ppermute(power_rows, "col", [(0, 1), (1, 0)])
    packed_gram = pair_gram(side.reshape(1), power_rows, other, edge)
    total_rows = power_rows.shape[0] * owners
    share = spread(packed_gram.reshape(owners, 1, -1), GROUPS).sum(0) / total_rows
    own = spread(jnp.broadcast_to(share, (owners,) + share.shape), CHIPS + ("col",))
    twin = lax.ppermute(own, "core", [(0, 1), (1, 0)])
    ids = jnp.stack([side, lax.axis_index("core")])
    half = (owners // 2, -1)
    return basis(ids, own.reshape(half), twin.reshape(half), power_rows, other)


def solution(mesh):
    owners, cols = mesh.devices.shape
    fine = Mesh(mesh.devices.reshape(owners // 16, 2, 4, 2, cols), GROUPS + ("col",))
    grouped = P(GROUPS)
    placed = (P(GROUPS, None, None), grouped, grouped, grouped, P(GROUPS, "col"), grouped)
    return jax.shard_map(
        local, mesh=fine, in_specs=placed, out_specs=P(GROUPS, "col"), check_vma=False
    )
```

```python
import jax
import jax.numpy as jnp
from jax import lax
from jax.experimental import pallas as pl
from jax.experimental.pallas import tpu as pltpu
from jax.sharding import Mesh
from jax.sharding import PartitionSpec as P

RB_DEV = 4
CHIPS = ("z", "y", "x")
GROUPS = CHIPS + ("core",)


def spread(rows, axes):
    return lax.all_to_all(rows, axes, split_axis=0, concat_axis=0, tiled=True)


SUB = 8
F32 = jnp.float32


def block_places():
    own = [((0, 0), (0, 1), (1, 1)), ((2, 2), (2, 3), (3, 3))]
    cross = [((0, 2), (1, 2)), ((0, 3), (1, 3))]
    return [place for side in range(2) for place in own[side] + cross[side]]


def pick(v, at):
    idx = jnp.full(v.shape, at, jnp.int32)
    return jnp.take_along_axis(v, idx, axis=1, mode='promise_in_bounds')


def eliminate(rows, edge, zero):
    lane = lax.broadcasted_iota(jnp.int32, (SUB, edge), 1)
    sub = lax.broadcasted_iota(jnp.int32, (SUB, edge), 0)
    rows = list(rows)
    last = len(rows)
    for g in range(last):
        base = g * SUB
        inside = (lane >= base) & (lane < base + SUB)
        start = jnp.where(inside, jnp.where(lane - base == sub, 1.0, 0.0), rows[g])
        wide_rows = [jnp.broadcast_to(rows[g][a : a + 1, :], (SUB, edge)) + zero for a in range(SUB)]
        s = {(a, c): pick(wide_rows[a], base + c) for a in range(SUB) for c in range(a, SUB)}
        x = [jnp.where(inside, jnp.where(lane == base + a, 1.0, 0.0), wide_rows[a]) for a in range(SUB)]
        r, low = [], {}
        ahead = g + 1 < last
        if ahead:
            nxt = rows[g + 1]
            fac = [jnp.broadcast_to(nxt[:, base + c : base + c + 1], (SUB, edge)) for c in range(SUB)]
            nxt = jnp.where(inside, 0.0, nxt)
        for a in range(SUB):
            r.append(lax.rsqrt(s[a, a]))
            for c in range(a + 1, SUB):
                low[c, a] = s[a, c] * r[a]
            for c in range(a + 1, SUB):
                for e in range(c, SUB):
                    s[c, e] = s[c, e] - low[c, a] * low[e, a]
            x[a] = x[a] * r[a]
            if ahead:
                fac[a] = fac[a] * r[a]
                nxt = nxt - fac[a] * x[a]
            for c in range(a + 1, SUB):
                x[c] = x[c] - low[c, a] * x[a]
                if ahead:
                    fac[c] = fac[c] - fac[a] * low[c, a]
        done = x[0]
        for a in range(1, SUB):
            done = jnp.where(sub == a, x[a], done)
        if g + 2 < last:
            z = [None] * SUB
            for a in range(SUB - 1, -1, -1):
                t = x[a]
                for c in range(a + 1, SUB):
                    t = t - low[c, a] * z[c]
                z[a] = t * r[a]
            for h in range(g + 2, last):
                old = rows[h]
                t = jnp.where(inside, 0.0, old)
                for a in range(SUB):
                    t = t - jnp.broadcast_to(old[:, base + a : base + a + 1], (SUB, edge)) * z[a]
                rows[h] = t
        if ahead:
            rows[g + 1] = nxt
        rows[g] = done
    return rows


def basis_body(
    side_ref, core_ref, own_ref, twin_ref, mine_ref, other_ref, out_ref, work_ref, inv_ref, row_ref, mix_ref, zero_ref
):
    edge, size = row_ref.shape
    count = size // edge
    hi = lax.Precision.HIGHEST
    side, core = side_ref[0], core_ref[0]
    zero_ref[...] = jnp.zeros(zero_ref.shape, F32)
    places = block_places()
    kinds = len(places) // 2
    part = edge // 2
    for n, (i, j) in enumerate(places):
        rows = pl.ds(n // kinds * part * kinds + n % kinds, part, kinds)
        mix_ref[pl.ds(n * edge + core, part, 2), :] = own_ref[rows, :]
        mix_ref[pl.ds(n * edge + 1 - core, part, 2), :] = twin_ref[rows, :]
        work_ref[i * edge : (i + 1) * edge, j * edge : (j + 1) * edge] = mix_ref[n * edge : (n + 1) * edge, :]
    everywhere = lax.broadcasted_iota(jnp.int32, (edge, size), 1)

    def stage(k, carry):
        base = pl.multiple_of(k * edge, edge)
        row_ref[...] = work_ref[pl.ds(base, edge), :]
        for n in range(1, count):

            @pl.when(k == n)
            def _():
                at = slice(n * edge, (n + 1) * edge)
                above = slice(0, n * edge)
                beyond = slice(n * edge, size)

                def product(ref, lanes):
                    return lax.dot_general(
                        work_ref[above, at], ref[above, lanes], (((0,), (0,)), ((), ())),
                        precision=hi, preferred_element_type=F32)

                row_ref[:, beyond] = row_ref[:, beyond] - product(work_ref, beyond)
                row_ref[:, above] = -product(inv_ref, above)

        rows = [row_ref[SUB * h : SUB * (h + 1), pl.ds(base, edge)] for h in range(edge // SUB)]
        w = jnp.concatenate(eliminate(rows, edge, zero_ref[...]), axis=0)
        r2 = lax.broadcasted_iota(jnp.int32, (edge, edge), 0)
        c2 = lax.broadcasted_iota(jnp.int32, (edge, edge), 1)
        inv = jnp.where(r2 >= c2, w, 0.0)
        done = jnp.dot(inv, row_ref[...], precision=hi, preferred_element_type=F32)
        work_ref[pl.ds(base, edge), :] = done
        inv_ref[pl.ds(base, edge), :] = jnp.where(everywhere < base, done, 0.0)
        inv_ref[pl.ds(base, edge), pl.ds(base, edge)] = inv
        return carry

    lax.fori_loop(0, count, stage, 0)
    width = mine_ref.shape[1]
    first = side == 0
    left = jnp.where(first, mine_ref[...], other_ref[...])
    right = jnp.where(first, other_ref[...], mine_ref[...])
    rest = inv_ref[pl.ds(pl.multiple_of(side * width, width), width), :]
    total = jnp.zeros(out_ref.shape, F32)
    for _ in range(3):
        step = rest.astype(jnp.bfloat16)
        rest = rest - step.astype(F32)
        for at, rows in ((0, left), (width, right)):
            total += lax.dot_general(
                rows, step[:, at : at + width], (((1,), (1,)), ((), ())), preferred_element_type=F32
            )
    out_ref[...] = total


def basis(side, core, own, twin, mine, other):
    edge, size = own.shape[1], 2 * mine.shape[1]
    scratch = [(size, size), (size, size), (edge, size), (2 * own.shape[0], edge), (SUB, edge)]
    return pl.pallas_call(
        basis_body,
        out_shape=jax.ShapeDtypeStruct(mine.shape, F32),
        in_specs=[pl.BlockSpec(memory_space=pltpu.SMEM)] * 2 + [pl.BlockSpec(memory_space=pltpu.VMEM)] * 4,
        out_specs=pl.BlockSpec(memory_space=pltpu.VMEM),
        scratch_shapes=[pltpu.VMEM(shape, F32) for shape in scratch],
    )(side, core, own, twin, mine, other)


def gram_body(side_ref, core_ref, mine_ref, other_ref, keep_ref, send_ref, mix_ref):
    edge = mix_ref.shape[1]
    first = side_ref[0] == 0
    core = core_ref[0]
    mine = mine_ref[...]
    other = other_ref[...]
    left = jnp.where(first, mine, other)
    right = jnp.where(first, other[:, :edge], mine[:, edge:])

    def product(a, b):
        return lax.dot_general(a, b, (((0,), (0,)), ((), ())), preferred_element_type=F32)

    own = product(mine, mine)
    cross = product(left, right)
    pieces = (own[:edge, :edge], own[:edge, edge:], own[edge:, edge:], cross[:edge], cross[edge:])
    kinds, part = len(pieces), edge // 2
    for n, piece in enumerate(pieces):
        mix_ref[n * edge : (n + 1) * edge, :] = piece
        keep_ref[pl.ds(n, part, kinds), :] = mix_ref[pl.ds(n * edge + core, part, 2), :]
        send_ref[pl.ds(n, part, kinds), :] = mix_ref[pl.ds(n * edge + 1 - core, part, 2), :]


def pair_gram(side, core, mine, other, edge):
    kinds = len(block_places()) // 2
    piece = jax.ShapeDtypeStruct((edge // 2 * kinds, edge), F32)
    return pl.pallas_call(
        gram_body,
        out_shape=(piece, piece),
        in_specs=[pl.BlockSpec(memory_space=pltpu.SMEM)] * 2 + [pl.BlockSpec(memory_space=pltpu.VMEM)] * 2,
        out_specs=(pl.BlockSpec(memory_space=pltpu.VMEM),) * 2,
        scratch_shapes=[pltpu.VMEM((kinds * edge, edge), F32)],
    )(side, core, mine, other)


def local(tiles, tile_rows, tile_cols, tile_count, sketch, variant_scale):
    slots, edge, _ = tiles.shape
    width = sketch.shape[1]
    owners = lax.axis_size(GROUPS)
    cols = lax.axis_size("col")
    own_blocks = sketch.shape[0] // edge
    blocks = owners * own_blocks
    bf16, f32 = jnp.bfloat16, jnp.float32

    own_rows = jnp.swapaxes(sketch.reshape(own_blocks, edge, width), 0, 1)
    own_scales = variant_scale.reshape(own_blocks, edge).T
    live = jnp.arange(slots, dtype=jnp.int32) < tile_count[0]
    run = jnp.where(live, tile_cols // own_blocks, -1).astype(bf16)
    member = (tile_cols % own_blocks).astype(bf16)
    notes = jnp.concatenate([run, member])
    notes = jnp.concatenate([own_scales, jnp.broadcast_to(notes, (edge, 2 * slots))], axis=1)
    notes = jnp.pad(notes, ((0, 0), (0, width - notes.shape[1])))
    packed = jnp.concatenate(
        [own_rows.reshape(edge, 2, -1), notes.reshape(edge, 2, -1)], axis=2
    )
    kept = spread(packed, GROUPS)
    row_part = own_blocks // 2 * width
    kept_rows = kept[:, :, :row_part].reshape(blocks, width)
    kept_notes = kept[:, :, row_part:].reshape(owners, width).astype(f32)
    kept_scale = kept_notes[:, :own_blocks].reshape(blocks, 1)
    all_runs = kept_notes[:, own_blocks : own_blocks + slots]
    all_members = kept_notes[:, own_blocks + slots : own_blocks + 2 * slots]
    all_cols = (all_runs * own_blocks + all_members).astype(jnp.int32)
    block_ids = jnp.arange(blocks, dtype=jnp.int32)
    picks = (all_cols[:, :, None] == block_ids).astype(bf16).reshape(owners * slots, blocks)

    row_ids = jnp.arange(RB_DEV, dtype=jnp.int32)
    row_mask = (tile_rows[:, None] == row_ids).astype(bf16)
    turned = jnp.transpose(tiles, (2, 0, 1))
    wide = turned[:, :, None, :] * row_mask[None, :, :, None]
    wide = wide.reshape(edge * slots, RB_DEV * edge)

    def forward(kept_operand):
        sent = jnp.dot(picks, kept_operand, preferred_element_type=f32).astype(bf16)
        fetched = spread(sent.reshape(owners, slots, width), GROUPS).reshape(edge * slots, width)
        return lax.dot_general(
            wide, fetched, (((0,), (0,)), ((), ())), preferred_element_type=f32
        ).astype(bf16)

    scaled = (kept_scale * kept_rows.astype(f32)).astype(bf16)
    squared = kept_scale * kept_scale
    range_rows, squared, gather_back = lax.optimization_barrier((forward(scaled), squared, picks))
    terms = jnp.dot(wide, range_rows, preferred_element_type=f32).astype(bf16)
    arrived = spread(terms.reshape(owners, slots, width), GROUPS).reshape(owners * slots, width)
    back = lax.dot_general(gather_back, arrived, (((0,), (0,)), ((), ())), preferred_element_type=f32)
    weighted = (squared * back).astype(bf16)
    power_rows = forward(lax.optimization_barrier(weighted))

    side = lax.axis_index("col").reshape(1)
    core = lax.axis_index("core").reshape(1)
    other = lax.ppermute(power_rows, "col", [(0, 1), (1, 0)])
    keep, send = pair_gram(side, core, power_rows, other, edge)
    total_rows = power_rows.shape[0] * owners
    chip = keep + lax.ppermute(send, "core", [(0, 1), (1, 0)])
    share = spread(chip.reshape(owners // 2, 1, -1), CHIPS).sum(0) / total_rows
    own = spread(jnp.broadcast_to(share, (owners,) + share.shape), ("col",) + CHIPS)
    twin = lax.ppermute(own, "core", [(0, 1), (1, 0)])
    return basis(side, core, own.reshape(-1, edge), twin.reshape(-1, edge), power_rows, other)


def solution(mesh):
    owners, cols = mesh.devices.shape
    fine = Mesh(mesh.devices.reshape(owners // 16, 2, 4, 2, cols), GROUPS + ("col",))
    grouped = P(GROUPS)
    placed = (P(GROUPS, None, None), grouped, grouped, grouped, P(GROUPS, "col"), grouped)
    return jax.shard_map(
        local, mesh=fine, in_specs=placed, out_specs=P(GROUPS, "col"), check_vma=False
    )
```

```python
import jax
import jax.numpy as jnp
from jax import lax
from jax.experimental import pallas as pl
from jax.experimental.pallas import tpu as pltpu
from jax.sharding import Mesh
from jax.sharding import PartitionSpec as P

RB_DEV = 4
CHIPS = ("z", "y", "x")
GROUPS = CHIPS + ("core",)


def spread(rows, axes):
    return lax.all_to_all(rows, axes, split_axis=0, concat_axis=0, tiled=True)


SUB = 8
F32 = jnp.float32


def block_places():
    own = [((0, 0), (0, 1), (1, 1)), ((2, 2), (2, 3), (3, 3))]
    cross = [((0, 2), (1, 2)), ((0, 3), (1, 3))]
    return [place for side in range(2) for place in own[side] + cross[side]]


def pick(v, at):
    idx = jnp.full(v.shape, at, jnp.int32)
    return jnp.take_along_axis(v, idx, axis=1, mode='promise_in_bounds')


def eliminate(rows, edge, zero):
    lane = lax.broadcasted_iota(jnp.int32, (SUB, edge), 1)
    sub = lax.broadcasted_iota(jnp.int32, (SUB, edge), 0)
    rows = list(rows)
    last = len(rows)
    for g in range(last):
        base = g * SUB
        inside = (lane >= base) & (lane < base + SUB)
        start = jnp.where(inside, jnp.where(lane - base == sub, 1.0, 0.0), rows[g])
        wide_rows = [jnp.broadcast_to(rows[g][a : a + 1, :], (SUB, edge)) + zero for a in range(SUB)]
        s = {(a, c): pick(wide_rows[a], base + c) for a in range(SUB) for c in range(a, SUB)}
        x = [jnp.where(inside, jnp.where(lane == base + a, 1.0, 0.0), wide_rows[a]) for a in range(SUB)]
        r, low = [], {}
        ahead = g + 1 < last
        if ahead:
            nxt = rows[g + 1]
            fac = [jnp.broadcast_to(nxt[:, base + c : base + c + 1], (SUB, edge)) for c in range(SUB)]
            nxt = jnp.where(inside, 0.0, nxt)
        for a in range(SUB):
            r.append(lax.rsqrt(s[a, a]))
            for c in range(a + 1, SUB):
                low[c, a] = s[a, c] * r[a]
            for c in range(a + 1, SUB):
                for e in range(c, SUB):
                    s[c, e] = s[c, e] - low[c, a] * low[e, a]
            x[a] = x[a] * r[a]
            if ahead:
                fac[a] = fac[a] * r[a]
                nxt = nxt - fac[a] * x[a]
            for c in range(a + 1, SUB):
                x[c] = x[c] - low[c, a] * x[a]
                if ahead:
                    fac[c] = fac[c] - fac[a] * low[c, a]
        done = x[0]
        for a in range(1, SUB):
            done = jnp.where(sub == a, x[a], done)
        if g + 2 < last:
            z = [None] * SUB
            for a in range(SUB - 1, -1, -1):
                t = x[a]
                for c in range(a + 1, SUB):
                    t = t - low[c, a] * z[c]
                z[a] = t * r[a]
            for h in range(g + 2, last):
                old = rows[h]
                t = jnp.where(inside, 0.0, old)
                for a in range(SUB):
                    t = t - jnp.broadcast_to(old[:, base + a : base + a + 1], (SUB, edge)) * z[a]
                rows[h] = t
        if ahead:
            rows[g + 1] = nxt
        rows[g] = done
    return rows


def basis_body(
    side_ref, core_ref, own_ref, twin_ref, mine_ref, other_ref, out_ref, work_ref, inv_ref, row_ref, mix_ref, zero_ref
):
    edge, size = row_ref.shape
    count = size // edge
    hi = lax.Precision.HIGHEST
    side, core = side_ref[0], core_ref[0]
    zero_ref[...] = jnp.zeros(zero_ref.shape, F32)
    places = block_places()
    kinds = len(places) // 2
    part = edge // 2
    for n, (i, j) in enumerate(places):
        rows = pl.ds(n // kinds * part * kinds + n % kinds, part, kinds)
        mix_ref[pl.ds(n * edge + core, part, 2), :] = own_ref[rows, :]
        mix_ref[pl.ds(n * edge + 1 - core, part, 2), :] = twin_ref[rows, :]
        work_ref[i * edge : (i + 1) * edge, j * edge : (j + 1) * edge] = mix_ref[n * edge : (n + 1) * edge, :]
    everywhere = lax.broadcasted_iota(jnp.int32, (edge, size), 1)

    def stage(k, carry):
        base = pl.multiple_of(k * edge, edge)
        row_ref[...] = work_ref[pl.ds(base, edge), :]
        for n in range(1, count):

            @pl.when(k == n)
            def _():
                at = slice(n * edge, (n + 1) * edge)
                above = slice(0, n * edge)
                beyond = slice(n * edge, size)

                def product(ref, lanes):
                    return lax.dot_general(
                        work_ref[above, at], ref[above, lanes], (((0,), (0,)), ((), ())),
                        precision=hi, preferred_element_type=F32)

                row_ref[:, beyond] = row_ref[:, beyond] - product(work_ref, beyond)
                row_ref[:, above] = -product(inv_ref, above)

        rows = [row_ref[SUB * h : SUB * (h + 1), pl.ds(base, edge)] for h in range(edge // SUB)]
        w = jnp.concatenate(eliminate(rows, edge, zero_ref[...]), axis=0)
        r2 = lax.broadcasted_iota(jnp.int32, (edge, edge), 0)
        c2 = lax.broadcasted_iota(jnp.int32, (edge, edge), 1)
        inv = jnp.where(r2 >= c2, w, 0.0)
        done = jnp.dot(inv, row_ref[...], precision=hi, preferred_element_type=F32)
        work_ref[pl.ds(base, edge), :] = done
        inv_ref[pl.ds(base, edge), :] = jnp.where(everywhere < base, done, 0.0)
        inv_ref[pl.ds(base, edge), pl.ds(base, edge)] = inv
        return carry

    lax.fori_loop(0, count, stage, 0)
    width = mine_ref.shape[1]
    first = side == 0
    left = jnp.where(first, mine_ref[...], other_ref[...])
    right = jnp.where(first, other_ref[...], mine_ref[...])
    rest = inv_ref[pl.ds(pl.multiple_of(side * width, width), width), :]
    total = jnp.zeros(out_ref.shape, F32)
    for _ in range(3):
        step = rest.astype(jnp.bfloat16)
        rest = rest - step.astype(F32)
        for at, rows in ((0, left), (width, right)):
            total += lax.dot_general(
                rows, step[:, at : at + width], (((1,), (1,)), ((), ())), preferred_element_type=F32
            )
    out_ref[...] = total


def basis(side, core, own, twin, mine, other):
    edge, size = own.shape[1], 2 * mine.shape[1]
    scratch = [(size, size), (size, size), (edge, size), (2 * own.shape[0], edge), (SUB, edge)]
    own, twin, mine, other = (pltpu.with_memory_space_constraint(v, pltpu.VMEM) for v in (own, twin, mine, other))
    return pl.pallas_call(
        basis_body,
        out_shape=jax.ShapeDtypeStruct(mine.shape, F32),
        in_specs=[pl.BlockSpec(memory_space=pltpu.SMEM)] * 2 + [pl.BlockSpec(memory_space=pltpu.VMEM)] * 4,
        out_specs=pl.BlockSpec(memory_space=pltpu.VMEM),
        scratch_shapes=[pltpu.VMEM(shape, F32) for shape in scratch],
    )(side, core, own, twin, mine, other)


def gram_body(side_ref, core_ref, mine_ref, other_ref, keep_ref, send_ref, mix_ref):
    edge = mix_ref.shape[1]
    first = side_ref[0] == 0
    core = core_ref[0]
    mine = mine_ref[...]
    other = other_ref[...]
    left = jnp.where(first, mine, other)
    right = jnp.where(first, other[:, :edge], mine[:, edge:])

    def product(a, b):
        return lax.dot_general(a, b, (((0,), (0,)), ((), ())), preferred_element_type=F32)

    own = product(mine, mine)
    cross = product(left, right)
    pieces = (own[:edge, :edge], own[:edge, edge:], own[edge:, edge:], cross[:edge], cross[edge:])
    kinds, part = len(pieces), edge // 2
    for n, piece in enumerate(pieces):
        mix_ref[n * edge : (n + 1) * edge, :] = piece
        keep_ref[pl.ds(n, part, kinds), :] = mix_ref[pl.ds(n * edge + core, part, 2), :]
        send_ref[pl.ds(n, part, kinds), :] = mix_ref[pl.ds(n * edge + 1 - core, part, 2), :]


def pair_gram(side, core, mine, other, edge):
    kinds = len(block_places()) // 2
    piece = pltpu.VMEM((edge // 2 * kinds, edge), F32)
    mine, other = (pltpu.with_memory_space_constraint(v, pltpu.VMEM) for v in (mine, other))
    return pl.pallas_call(
        gram_body,
        out_shape=(piece, piece),
        in_specs=[pl.BlockSpec(memory_space=pltpu.SMEM)] * 2 + [pl.BlockSpec(memory_space=pltpu.VMEM)] * 2,
        out_specs=(pl.BlockSpec(memory_space=pltpu.VMEM),) * 2,
        scratch_shapes=[pltpu.VMEM((kinds * edge, edge), F32)],
    )(side, core, mine, other)


def local(tiles, tile_rows, tile_cols, tile_count, sketch, variant_scale):
    slots, edge, _ = tiles.shape
    width = sketch.shape[1]
    owners = lax.axis_size(GROUPS)
    cols = lax.axis_size("col")
    own_blocks = sketch.shape[0] // edge
    blocks = owners * own_blocks
    bf16, f32 = jnp.bfloat16, jnp.float32

    own_rows = jnp.swapaxes(sketch.reshape(own_blocks, edge, width), 0, 1)
    own_scales = variant_scale.reshape(own_blocks, edge).T
    live = jnp.arange(slots, dtype=jnp.int32) < tile_count[0]
    run = jnp.where(live, tile_cols // own_blocks, -1).astype(bf16)
    member = (tile_cols % own_blocks).astype(bf16)
    notes = jnp.concatenate([run, member])
    notes = jnp.concatenate([own_scales, jnp.broadcast_to(notes, (edge, 2 * slots))], axis=1)
    notes = jnp.pad(notes, ((0, 0), (0, width - notes.shape[1])))
    packed = jnp.concatenate(
        [own_rows.reshape(edge, 2, -1), notes.reshape(edge, 2, -1)], axis=2
    )
    row_ids = jnp.arange(RB_DEV, dtype=jnp.int32)
    row_mask = (tile_rows[:, None] == row_ids).astype(bf16)
    turned = jnp.transpose(tiles, (2, 0, 1))
    wide = turned[:, :, None, :] * row_mask[None, :, :, None]
    wide = wide.reshape(edge * slots, RB_DEV * edge)
    kept, wide = lax.optimization_barrier((spread(packed, GROUPS), wide))
    row_part = own_blocks // 2 * width
    kept_rows = kept[:, :, :row_part].reshape(blocks, width)
    kept_notes = kept[:, :, row_part:].reshape(owners, width).astype(f32)
    kept_scale = kept_notes[:, :own_blocks].reshape(blocks, 1)
    all_runs = kept_notes[:, own_blocks : own_blocks + slots]
    all_members = kept_notes[:, own_blocks + slots : own_blocks + 2 * slots]
    all_cols = (all_runs * own_blocks + all_members).astype(jnp.int32)
    block_ids = jnp.arange(blocks, dtype=jnp.int32)
    picks = (all_cols[:, :, None] == block_ids).astype(bf16).reshape(owners * slots, blocks)
    squared = kept_scale * kept_scale
    picks, squared = lax.optimization_barrier((picks, squared))

    def forward(kept_operand):
        sent = jnp.dot(picks, kept_operand, preferred_element_type=f32).astype(bf16)
        fetched = spread(sent.reshape(owners, slots, width), GROUPS).reshape(edge * slots, width)
        return lax.dot_general(
            wide, fetched, (((0,), (0,)), ((), ())), preferred_element_type=f32
        ).astype(bf16)

    scaled = (kept_scale * kept_rows.astype(f32)).astype(bf16)
    range_rows = lax.optimization_barrier(forward(scaled))
    terms = jnp.dot(wide, range_rows, preferred_element_type=f32).astype(bf16)
    arrived = spread(terms.reshape(owners, slots, width), GROUPS).reshape(owners * slots, width)
    back = lax.dot_general(picks, arrived, (((0,), (0,)), ((), ())), preferred_element_type=f32)
    weighted = (squared * back).astype(bf16)
    power_rows = forward(lax.optimization_barrier(weighted))

    side = lax.axis_index("col").reshape(1)
    core = lax.axis_index("core").reshape(1)
    other = lax.ppermute(power_rows, "col", [(0, 1), (1, 0)])
    keep, send = pair_gram(side, core, power_rows, other, edge)
    total_rows = power_rows.shape[0] * owners
    chip = keep + lax.ppermute(send, "core", [(0, 1), (1, 0)])
    share = spread(chip.reshape(owners // 2, 1, -1), CHIPS).sum(0) / total_rows
    own = spread(jnp.broadcast_to(share, (owners,) + share.shape), ("col",) + CHIPS)
    twin = lax.ppermute(own, "core", [(0, 1), (1, 0)])
    return basis(side, core, own.reshape(-1, edge), twin.reshape(-1, edge), power_rows, other)


def solution(mesh):
    owners, cols = mesh.devices.shape
    fine = Mesh(mesh.devices.reshape(owners // 16, 2, 4, 2, cols), GROUPS + ("col",))
    grouped = P(GROUPS)
    placed = (P(GROUPS, None, None), grouped, grouped, grouped, P(GROUPS, "col"), grouped)
    return jax.shard_map(
        local, mesh=fine, in_specs=placed, out_specs=P(GROUPS, "col"), check_vma=False
    )
```

```python
import jax
import jax.numpy as jnp
from jax import lax
from jax.experimental import pallas as pl
from jax.experimental.pallas import tpu as pltpu
from jax.sharding import Mesh
from jax.sharding import PartitionSpec as P

RB_DEV = 4
CHIPS = ("z", "y", "x")
GROUPS = CHIPS + ("core",)


def spread(rows, axes):
    return lax.all_to_all(rows, axes, split_axis=0, concat_axis=0, tiled=True)


SUB = 8
F32 = jnp.float32


def block_places():
    own = [((0, 0), (0, 1), (1, 1)), ((2, 2), (2, 3), (3, 3))]
    cross = [((0, 2), (1, 2)), ((0, 3), (1, 3))]
    return [place for side in range(2) for place in own[side] + cross[side]]


def pick(v, at):
    idx = jnp.full(v.shape, at, jnp.int32)
    return jnp.take_along_axis(v, idx, axis=1, mode='promise_in_bounds')


def eliminate(rows, edge, zero):
    lane = lax.broadcasted_iota(jnp.int32, (SUB, edge), 1)
    sub = lax.broadcasted_iota(jnp.int32, (SUB, edge), 0)
    rows = list(rows)
    last = len(rows)
    for g in range(last):
        base = g * SUB
        inside = (lane >= base) & (lane < base + SUB)
        start = jnp.where(inside, jnp.where(lane - base == sub, 1.0, 0.0), rows[g])
        wide_rows = [jnp.broadcast_to(rows[g][a : a + 1, :], (SUB, edge)) + zero for a in range(SUB)]
        s = {(a, c): pick(wide_rows[a], base + c) for a in range(SUB) for c in range(a, SUB)}
        x = [jnp.where(inside, jnp.where(lane == base + a, 1.0, 0.0), wide_rows[a]) for a in range(SUB)]
        r, low = [], {}
        ahead = g + 1 < last
        if ahead:
            nxt = rows[g + 1]
            fac = [jnp.broadcast_to(nxt[:, base + c : base + c + 1], (SUB, edge)) for c in range(SUB)]
            nxt = jnp.where(inside, 0.0, nxt)
        for a in range(SUB):
            r.append(lax.rsqrt(s[a, a]))
            for c in range(a + 1, SUB):
                low[c, a] = s[a, c] * r[a]
            for c in range(a + 1, SUB):
                for e in range(c, SUB):
                    s[c, e] = s[c, e] - low[c, a] * low[e, a]
            x[a] = x[a] * r[a]
            if ahead:
                fac[a] = fac[a] * r[a]
                nxt = nxt - fac[a] * x[a]
            for c in range(a + 1, SUB):
                x[c] = x[c] - low[c, a] * x[a]
                if ahead:
                    fac[c] = fac[c] - fac[a] * low[c, a]
        done = x[0]
        for a in range(1, SUB):
            done = jnp.where(sub == a, x[a], done)
        if g + 2 < last:
            z = [None] * SUB
            for a in range(SUB - 1, -1, -1):
                t = x[a]
                for c in range(a + 1, SUB):
                    t = t - low[c, a] * z[c]
                z[a] = t * r[a]
            for h in range(g + 2, last):
                old = rows[h]
                t = jnp.where(inside, 0.0, old)
                for a in range(SUB):
                    t = t - jnp.broadcast_to(old[:, base + a : base + a + 1], (SUB, edge)) * z[a]
                rows[h] = t
        if ahead:
            rows[g + 1] = nxt
        rows[g] = done
    return rows


def basis_body(
    side_ref, core_ref, own_ref, twin_ref, mine_ref, other_ref, out_ref, work_ref, inv_ref, row_ref, mix_ref, zero_ref
):
    edge, size = row_ref.shape
    count = size // edge
    hi = lax.Precision.HIGHEST
    side, core = side_ref[0], core_ref[0]
    zero_ref[...] = jnp.zeros(zero_ref.shape, F32)
    places = block_places()
    kinds = len(places) // 2
    part = edge // 2
    for n, (i, j) in enumerate(places):
        rows = pl.ds(n // kinds * part * kinds + n % kinds, part, kinds)
        mix_ref[pl.ds(n * edge + core, part, 2), :] = own_ref[rows, :]
        mix_ref[pl.ds(n * edge + 1 - core, part, 2), :] = twin_ref[rows, :]
        work_ref[i * edge : (i + 1) * edge, j * edge : (j + 1) * edge] = mix_ref[n * edge : (n + 1) * edge, :]
    everywhere = lax.broadcasted_iota(jnp.int32, (edge, size), 1)

    def stage(k, carry):
        base = pl.multiple_of(k * edge, edge)
        row_ref[...] = work_ref[pl.ds(base, edge), :]
        for n in range(1, count):

            @pl.when(k == n)
            def _():
                at = slice(n * edge, (n + 1) * edge)
                above = slice(0, n * edge)
                beyond = slice(n * edge, size)

                def product(ref, lanes):
                    return lax.dot_general(
                        work_ref[above, at], ref[above, lanes], (((0,), (0,)), ((), ())),
                        precision=hi, preferred_element_type=F32)

                row_ref[:, beyond] = row_ref[:, beyond] - product(work_ref, beyond)
                row_ref[:, above] = -product(inv_ref, above)

        rows = [row_ref[SUB * h : SUB * (h + 1), pl.ds(base, edge)] for h in range(edge // SUB)]
        w = jnp.concatenate(eliminate(rows, edge, zero_ref[...]), axis=0)
        r2 = lax.broadcasted_iota(jnp.int32, (edge, edge), 0)
        c2 = lax.broadcasted_iota(jnp.int32, (edge, edge), 1)
        inv = jnp.where(r2 >= c2, w, 0.0)
        done = jnp.dot(inv, row_ref[...], precision=hi, preferred_element_type=F32)
        work_ref[pl.ds(base, edge), :] = done
        inv_ref[pl.ds(base, edge), :] = jnp.where(everywhere < base, done, 0.0)
        inv_ref[pl.ds(base, edge), pl.ds(base, edge)] = inv
        return carry

    lax.fori_loop(0, count, stage, 0)
    width = mine_ref.shape[1]
    first = side == 0
    left = jnp.where(first, mine_ref[...], other_ref[...])
    right = jnp.where(first, other_ref[...], mine_ref[...])
    rest = inv_ref[pl.ds(pl.multiple_of(side * width, width), width), :]
    total = jnp.zeros(out_ref.shape, F32)
    for _ in range(3):
        step = rest.astype(jnp.bfloat16)
        rest = rest - step.astype(F32)
        for at, rows in ((0, left), (width, right)):
            total += lax.dot_general(
                rows, step[:, at : at + width], (((1,), (1,)), ((), ())), preferred_element_type=F32
            )
    out_ref[...] = total


def basis(side, core, own, twin, mine, other):
    edge, size = own.shape[1], 2 * mine.shape[1]
    scratch = [(size, size), (size, size), (edge, size), (2 * own.shape[0], edge), (SUB, edge)]
    own, twin, mine, other = (pltpu.with_memory_space_constraint(v, pltpu.VMEM) for v in (own, twin, mine, other))
    return pl.pallas_call(
        basis_body,
        out_shape=jax.ShapeDtypeStruct(mine.shape, F32),
        in_specs=[pl.BlockSpec(memory_space=pltpu.SMEM)] * 2 + [pl.BlockSpec(memory_space=pltpu.VMEM)] * 4,
        out_specs=pl.BlockSpec(memory_space=pltpu.VMEM),
        scratch_shapes=[pltpu.VMEM(shape, F32) for shape in scratch],
    )(side, core, own, twin, mine, other)


def gram_body(side_ref, core_ref, mine_ref, other_ref, keep_ref, send_ref, mix_ref):
    edge = mix_ref.shape[1]
    first = side_ref[0] == 0
    core = core_ref[0]
    mine = mine_ref[...]
    other = other_ref[...]
    left = jnp.where(first, mine, other)
    right = jnp.where(first, other[:, :edge], mine[:, edge:])

    def product(a, b):
        return lax.dot_general(a, b, (((0,), (0,)), ((), ())), preferred_element_type=F32)

    own = product(mine, mine)
    cross = product(left, right)
    pieces = (own[:edge, :edge], own[:edge, edge:], own[edge:, edge:], cross[:edge], cross[edge:])
    kinds, part = len(pieces), edge // 2
    for n, piece in enumerate(pieces):
        mix_ref[n * edge : (n + 1) * edge, :] = piece
        keep_ref[pl.ds(n, part, kinds), :] = mix_ref[pl.ds(n * edge + core, part, 2), :]
        send_ref[pl.ds(n, part, kinds), :] = mix_ref[pl.ds(n * edge + 1 - core, part, 2), :]


def pair_gram(side, core, mine, other, edge):
    kinds = len(block_places()) // 2
    piece = pltpu.VMEM((edge // 2 * kinds, edge), F32)
    mine, other = (pltpu.with_memory_space_constraint(v, pltpu.VMEM) for v in (mine, other))
    return pl.pallas_call(
        gram_body,
        out_shape=(piece, piece),
        in_specs=[pl.BlockSpec(memory_space=pltpu.SMEM)] * 2 + [pl.BlockSpec(memory_space=pltpu.VMEM)] * 2,
        out_specs=(pl.BlockSpec(memory_space=pltpu.VMEM),) * 2,
        scratch_shapes=[pltpu.VMEM((kinds * edge, edge), F32)],
    )(side, core, mine, other)


def local(tiles, tile_rows, tile_cols, tile_count, sketch, variant_scale):
    slots, edge, _ = tiles.shape
    width = sketch.shape[1]
    owners = lax.axis_size(GROUPS)
    cols = lax.axis_size("col")
    own_blocks = sketch.shape[0] // edge
    blocks = owners * own_blocks
    bf16, f32 = jnp.bfloat16, jnp.float32

    scaled = (variant_scale.astype(f32)[:, None] * sketch.astype(f32)).astype(bf16)
    own_rows = jnp.swapaxes(scaled.reshape(own_blocks, edge, width), 0, 1)
    own_scales = variant_scale.reshape(own_blocks, edge).T
    live = jnp.arange(slots, dtype=jnp.int32) < tile_count[0]
    run = jnp.where(live, tile_cols // own_blocks, -1).astype(bf16)
    member = (tile_cols % own_blocks).astype(bf16)
    notes = jnp.concatenate([run, member])
    notes = jnp.concatenate([own_scales, jnp.broadcast_to(notes, (edge, 2 * slots))], axis=1)
    notes = jnp.pad(notes, ((0, 0), (0, width - notes.shape[1])))
    packed = jnp.concatenate(
        [own_rows.reshape(edge, 2, -1), notes.reshape(edge, 2, -1)], axis=2
    )
    row_ids = jnp.arange(RB_DEV, dtype=jnp.int32)
    row_mask = (tile_rows[:, None] == row_ids).astype(bf16)
    turned = jnp.transpose(tiles, (2, 0, 1))
    wide = turned[:, :, None, :] * row_mask[None, :, :, None]
    wide = wide.reshape(edge * slots, RB_DEV * edge)
    kept = spread(packed, GROUPS)
    row_part = own_blocks // 2 * width
    kept_rows = kept[:, :, :row_part].reshape(blocks, width)
    kept_notes = kept[:, :, row_part:].reshape(owners, width).astype(f32)
    kept_scale = kept_notes[:, :own_blocks].reshape(blocks, 1)
    all_runs = kept_notes[:, own_blocks : own_blocks + slots]
    all_members = kept_notes[:, own_blocks + slots : own_blocks + 2 * slots]
    all_cols = (all_runs * own_blocks + all_members).astype(jnp.int32)
    block_ids = jnp.arange(blocks, dtype=jnp.int32)
    picks = (all_cols[:, :, None] == block_ids).astype(bf16).reshape(owners * slots, blocks)
    squared = kept_scale * kept_scale
    picks, squared, wide = lax.optimization_barrier((picks, squared, wide))

    def forward(kept_operand):
        sent = jnp.dot(picks, kept_operand, preferred_element_type=f32).astype(bf16)
        fetched = spread(sent.reshape(owners, slots, width), GROUPS).reshape(edge * slots, width)
        return lax.dot_general(
            wide, fetched, (((0,), (0,)), ((), ())), preferred_element_type=f32
        ).astype(bf16)

    range_rows = lax.optimization_barrier(forward(kept_rows))
    terms = jnp.dot(wide, range_rows, preferred_element_type=f32).astype(bf16)
    arrived = spread(terms.reshape(owners, slots, width), GROUPS).reshape(owners * slots, width)
    back = lax.dot_general(picks, arrived, (((0,), (0,)), ((), ())), preferred_element_type=f32)
    weighted = (squared * back).astype(bf16)
    power_rows = forward(lax.optimization_barrier(weighted))

    side = lax.axis_index("col").reshape(1)
    core = lax.axis_index("core").reshape(1)
    other = lax.ppermute(power_rows, "col", [(0, 1), (1, 0)])
    keep, send = pair_gram(side, core, power_rows, other, edge)
    total_rows = power_rows.shape[0] * owners
    chip = keep + lax.ppermute(send, "core", [(0, 1), (1, 0)])
    share = spread(chip.reshape(owners // 2, 1, -1), CHIPS).sum(0) / total_rows
    own = spread(jnp.broadcast_to(share, (owners,) + share.shape), ("col",) + CHIPS)
    twin = lax.ppermute(own, "core", [(0, 1), (1, 0)])
    return basis(side, core, own.reshape(-1, edge), twin.reshape(-1, edge), power_rows, other)


def solution(mesh):
    owners, cols = mesh.devices.shape
    fine = Mesh(mesh.devices.reshape(owners // 16, 2, 4, 2, cols), GROUPS + ("col",))
    grouped = P(GROUPS)
    placed = (P(GROUPS, None, None), grouped, grouped, grouped, P(GROUPS, "col"), grouped)
    return jax.shard_map(
        local, mesh=fine, in_specs=placed, out_specs=P(GROUPS, "col"), check_vma=False
    )
```

```python
import jax
import jax.numpy as jnp
from jax import lax
from jax.experimental import pallas as pl
from jax.experimental.pallas import tpu as pltpu
from jax.sharding import Mesh
from jax.sharding import PartitionSpec as P

RB_DEV = 4
CHIPS = ("z", "y", "x")
GROUPS = CHIPS + ("core",)


def spread(rows, axes):
    return lax.all_to_all(rows, axes, split_axis=0, concat_axis=0, tiled=True)


SUB = 8
F32 = jnp.float32


def block_places():
    own = [((0, 0), (0, 1), (1, 1)), ((2, 2), (2, 3), (3, 3))]
    cross = [((0, 2), (1, 2)), ((0, 3), (1, 3))]
    return [place for side in range(2) for place in own[side] + cross[side]]


def pick(v, at):
    idx = jnp.full(v.shape, at, jnp.int32)
    return jnp.take_along_axis(v, idx, axis=1, mode='promise_in_bounds')


def eliminate(rows, edge, zero):
    lane = lax.broadcasted_iota(jnp.int32, (SUB, edge), 1)
    sub = lax.broadcasted_iota(jnp.int32, (SUB, edge), 0)
    rows = list(rows)
    last = len(rows)
    for g in range(last):
        base = g * SUB
        inside = (lane >= base) & (lane < base + SUB)
        start = jnp.where(inside, jnp.where(lane - base == sub, 1.0, 0.0), rows[g])
        wide_rows = [jnp.broadcast_to(rows[g][a : a + 1, :], (SUB, edge)) + zero for a in range(SUB)]
        s = {(a, c): pick(wide_rows[a], base + c) for a in range(SUB) for c in range(a, SUB)}
        x = [jnp.where(inside, jnp.where(lane == base + a, 1.0, 0.0), wide_rows[a]) for a in range(SUB)]
        r, low = [], {}
        ahead = g + 1 < last
        if ahead:
            nxt = rows[g + 1]
            fac = [jnp.broadcast_to(nxt[:, base + c : base + c + 1], (SUB, edge)) for c in range(SUB)]
            nxt = jnp.where(inside, 0.0, nxt)
        for a in range(SUB):
            r.append(lax.rsqrt(s[a, a]))
            for c in range(a + 1, SUB):
                low[c, a] = s[a, c] * r[a]
            for c in range(a + 1, SUB):
                for e in range(c, SUB):
                    s[c, e] = s[c, e] - low[c, a] * low[e, a]
            x[a] = x[a] * r[a]
            if ahead:
                fac[a] = fac[a] * r[a]
                nxt = nxt - fac[a] * x[a]
            for c in range(a + 1, SUB):
                x[c] = x[c] - low[c, a] * x[a]
                if ahead:
                    fac[c] = fac[c] - fac[a] * low[c, a]
        done = x[0]
        for a in range(1, SUB):
            done = jnp.where(sub == a, x[a], done)
        if g + 2 < last:
            z = [None] * SUB
            for a in range(SUB - 1, -1, -1):
                t = x[a]
                for c in range(a + 1, SUB):
                    t = t - low[c, a] * z[c]
                z[a] = t * r[a]
            for h in range(g + 2, last):
                old = rows[h]
                t = jnp.where(inside, 0.0, old)
                for a in range(SUB):
                    t = t - jnp.broadcast_to(old[:, base + a : base + a + 1], (SUB, edge)) * z[a]
                rows[h] = t
        if ahead:
            rows[g + 1] = nxt
        rows[g] = done
    return rows


def basis_body(
    side_ref, core_ref, own_ref, twin_ref, mine_ref, other_ref, out_ref, work_ref, inv_ref, row_ref, mix_ref, zero_ref
):
    edge, size = row_ref.shape
    count = size // edge
    hi = lax.Precision.HIGHEST
    side, core = side_ref[0], core_ref[0]
    zero_ref[...] = jnp.zeros(zero_ref.shape, F32)
    places = block_places()
    kinds = len(places) // 2
    part = edge // 2
    for n, (i, j) in enumerate(places):
        rows = pl.ds(n // kinds * part * kinds + n % kinds, part, kinds)
        mix_ref[pl.ds(n * edge + core, part, 2), :] = own_ref[rows, :]
        mix_ref[pl.ds(n * edge + 1 - core, part, 2), :] = twin_ref[rows, :]
        work_ref[i * edge : (i + 1) * edge, j * edge : (j + 1) * edge] = mix_ref[n * edge : (n + 1) * edge, :]
    everywhere = lax.broadcasted_iota(jnp.int32, (edge, size), 1)

    def stage(k, carry):
        base = pl.multiple_of(k * edge, edge)
        row_ref[...] = work_ref[pl.ds(base, edge), :]
        for n in range(1, count):

            @pl.when(k == n)
            def _():
                at = slice(n * edge, (n + 1) * edge)
                above = slice(0, n * edge)
                beyond = slice(n * edge, size)

                def product(ref, lanes):
                    return lax.dot_general(
                        work_ref[above, at], ref[above, lanes], (((0,), (0,)), ((), ())),
                        precision=hi, preferred_element_type=F32)

                row_ref[:, beyond] = row_ref[:, beyond] - product(work_ref, beyond)
                row_ref[:, above] = -product(inv_ref, above)

        rows = [row_ref[SUB * h : SUB * (h + 1), pl.ds(base, edge)] for h in range(edge // SUB)]
        w = jnp.concatenate(eliminate(rows, edge, zero_ref[...]), axis=0)
        r2 = lax.broadcasted_iota(jnp.int32, (edge, edge), 0)
        c2 = lax.broadcasted_iota(jnp.int32, (edge, edge), 1)
        inv = jnp.where(r2 >= c2, w, 0.0)
        done = jnp.dot(inv, row_ref[...], precision=hi, preferred_element_type=F32)
        work_ref[pl.ds(base, edge), :] = done
        inv_ref[pl.ds(base, edge), :] = jnp.where(everywhere < base, done, 0.0)
        inv_ref[pl.ds(base, edge), pl.ds(base, edge)] = inv
        return carry

    lax.fori_loop(0, count, stage, 0)
    width = mine_ref.shape[1]
    first = side == 0
    left = jnp.where(first, mine_ref[...], other_ref[...])
    right = jnp.where(first, other_ref[...], mine_ref[...])
    rest = inv_ref[pl.ds(pl.multiple_of(side * width, width), width), :]
    total = jnp.zeros(out_ref.shape, F32)
    for _ in range(3):
        step = rest.astype(jnp.bfloat16)
        rest = rest - step.astype(F32)
        for at, rows in ((0, left), (width, right)):
            total += lax.dot_general(
                rows, step[:, at : at + width], (((1,), (1,)), ((), ())), preferred_element_type=F32
            )
    out_ref[...] = total


def basis(side, core, own, twin, mine, other):
    edge, size = own.shape[1], 2 * mine.shape[1]
    scratch = [(size, size), (size, size), (edge, size), (2 * own.shape[0], edge), (SUB, edge)]
    own, twin, mine, other = (pltpu.with_memory_space_constraint(v, pltpu.VMEM) for v in (own, twin, mine, other))
    return pl.pallas_call(
        basis_body,
        out_shape=jax.ShapeDtypeStruct(mine.shape, F32),
        in_specs=[pl.BlockSpec(memory_space=pltpu.SMEM)] * 2 + [pl.BlockSpec(memory_space=pltpu.VMEM)] * 4,
        out_specs=pl.BlockSpec(memory_space=pltpu.VMEM),
        scratch_shapes=[pltpu.VMEM(shape, F32) for shape in scratch],
    )(side, core, own, twin, mine, other)


def gram_body(side_ref, core_ref, mine_ref, other_ref, keep_ref, send_ref, mix_ref):
    edge = mix_ref.shape[1]
    first = side_ref[0] == 0
    core = core_ref[0]
    mine = mine_ref[...]
    other = other_ref[...]
    left = jnp.where(first, mine, other)
    right = jnp.where(first, other[:, :edge], mine[:, edge:])

    def product(a, b):
        return lax.dot_general(a, b, (((0,), (0,)), ((), ())), preferred_element_type=F32)

    own = product(mine, mine)
    cross = product(left, right)
    pieces = (own[:edge, :edge], own[:edge, edge:], own[edge:, edge:], cross[:edge], cross[edge:])
    kinds, part = len(pieces), edge // 2
    for n, piece in enumerate(pieces):
        mix_ref[n * edge : (n + 1) * edge, :] = piece
        keep_ref[pl.ds(n, part, kinds), :] = mix_ref[pl.ds(n * edge + core, part, 2), :]
        send_ref[pl.ds(n, part, kinds), :] = mix_ref[pl.ds(n * edge + 1 - core, part, 2), :]


def pair_gram(side, core, mine, other, edge):
    kinds = len(block_places()) // 2
    piece = pltpu.VMEM((edge // 2 * kinds, edge), F32)
    mine, other = (pltpu.with_memory_space_constraint(v, pltpu.VMEM) for v in (mine, other))
    return pl.pallas_call(
        gram_body,
        out_shape=(piece, piece),
        in_specs=[pl.BlockSpec(memory_space=pltpu.SMEM)] * 2 + [pl.BlockSpec(memory_space=pltpu.VMEM)] * 2,
        out_specs=(pl.BlockSpec(memory_space=pltpu.VMEM),) * 2,
        scratch_shapes=[pltpu.VMEM((kinds * edge, edge), F32)],
    )(side, core, mine, other)


def local(tiles, tile_rows, tile_cols, tile_count, sketch, variant_scale):
    slots, edge, _ = tiles.shape
    width = sketch.shape[1]
    owners = lax.axis_size(GROUPS)
    cols = lax.axis_size("col")
    own_blocks = sketch.shape[0] // edge
    blocks = owners * own_blocks
    bf16, f32 = jnp.bfloat16, jnp.float32

    scaled = (variant_scale.astype(f32)[:, None] * sketch.astype(f32)).astype(bf16)
    own_rows = jnp.swapaxes(scaled.reshape(own_blocks, edge, width), 0, 1)
    own_scales = variant_scale.reshape(own_blocks, edge).T
    live = jnp.arange(slots, dtype=jnp.int32) < tile_count[0]
    run = jnp.where(live, tile_cols // own_blocks, -1).astype(bf16)
    member = (tile_cols % own_blocks).astype(bf16)
    notes = jnp.concatenate([run, member])
    notes = jnp.concatenate([own_scales, jnp.broadcast_to(notes, (edge, 2 * slots))], axis=1)
    notes = jnp.pad(notes, ((0, 0), (0, width - notes.shape[1])))
    packed = jnp.concatenate(
        [own_rows.reshape(edge, 2, -1), notes.reshape(edge, 2, -1)], axis=2
    )
    row_ids = jnp.arange(RB_DEV, dtype=jnp.int32)
    row_mask = (tile_rows[:, None] == row_ids).astype(bf16)
    turned = jnp.transpose(tiles, (2, 0, 1))
    wide = turned[:, :, None, :] * row_mask[None, :, :, None]
    wide = wide.reshape(edge * slots, RB_DEV * edge)
    kept = spread(packed, GROUPS)
    row_part = own_blocks // 2 * width
    kept_rows = kept[:, :, :row_part].reshape(owners, own_blocks, width)
    kept_rows = jnp.swapaxes(kept_rows, 0, 1).reshape(blocks, width)
    kept_notes = kept[:, :, row_part:].reshape(owners, width).astype(f32)
    kept_scale = kept_notes[:, :own_blocks].T.reshape(blocks, 1)
    all_runs = kept_notes[:, own_blocks : own_blocks + slots]
    all_members = kept_notes[:, own_blocks + slots : own_blocks + 2 * slots]
    all_cols = jnp.where(all_runs < 0, -1, all_members * owners + all_runs).astype(jnp.int32)
    block_ids = jnp.arange(blocks, dtype=jnp.int32)
    picks = (all_cols[:, :, None] == block_ids).astype(bf16).reshape(owners * slots, blocks)
    squared = kept_scale * kept_scale
    picks, squared, wide = lax.optimization_barrier((picks, squared, wide))

    def forward(kept_operand):
        sent = jnp.dot(picks, kept_operand, preferred_element_type=f32).astype(bf16)
        fetched = spread(sent.reshape(owners, slots, width), GROUPS).reshape(edge * slots, width)
        return lax.dot_general(
            wide, fetched, (((0,), (0,)), ((), ())), preferred_element_type=f32
        ).astype(bf16)

    range_rows = lax.optimization_barrier(forward(kept_rows))
    terms = jnp.dot(wide, range_rows, preferred_element_type=f32).astype(bf16)
    arrived = spread(terms.reshape(owners, slots, width), GROUPS).reshape(owners * slots, width)
    back = lax.dot_general(picks, arrived, (((0,), (0,)), ((), ())), preferred_element_type=f32)
    weighted = (squared * back).astype(bf16)
    power_rows = forward(lax.optimization_barrier(weighted))

    side = lax.axis_index("col").reshape(1)
    core = lax.axis_index("core").reshape(1)
    other = lax.ppermute(power_rows, "col", [(0, 1), (1, 0)])
    keep, send = pair_gram(side, core, power_rows, other, edge)
    total_rows = power_rows.shape[0] * owners
    chip = keep + lax.ppermute(send, "core", [(0, 1), (1, 0)])
    share = spread(chip.reshape(owners // 2, 1, -1), CHIPS).sum(0) / total_rows
    own = spread(jnp.broadcast_to(share, (owners,) + share.shape), ("col",) + CHIPS)
    twin = lax.ppermute(own, "core", [(0, 1), (1, 0)])
    return basis(side, core, own.reshape(-1, edge), twin.reshape(-1, edge), power_rows, other)


def solution(mesh):
    owners, cols = mesh.devices.shape
    fine = Mesh(mesh.devices.reshape(owners // 16, 2, 4, 2, cols), GROUPS + ("col",))
    grouped = P(GROUPS)
    placed = (P(GROUPS, None, None), grouped, grouped, grouped, P(GROUPS, "col"), grouped)
    return jax.shard_map(
        local, mesh=fine, in_specs=placed, out_specs=P(GROUPS, "col"), check_vma=False
    )
```
